512 devices in a mesh: row: 16 (over z), col: 32 (over x, y, core).
Axes of the slice: x: 4, y: 4, z: 16, core: 2. Of those that a mesh axis runs over, the one named last changes fastest.
Arguments:
- operator_tiles: bfloat16 [64, 128, 9, 64, 64], P('row', 'col'), may hold values from -0.25 to 0.25
- neighbour_codes: int32 [64, 128, 9], P('row', 'col'), may hold values from 0 to 8, as said below
- live_slots: int32 [64, 128], P('row', 'col'), may hold values from 1 to 9, as said below
- prolong_tiles: bfloat16 [64, 128, 6, 64, 64], P('row', 'col'), may hold values from -0.75 to 0.75
- coarse_blocks: int32 [64, 128, 6], P('row', 'col'), may hold values from 0 to 127, as said below
Outputs:
- coarse_band: float32 [32, 256, 1792], P('col', 'row')
The draws below stay inside these ranges and needn't reach their ends.
Inputs may be any that keep to these rules, and one draw needn't show every extreme that they name: `neighbour_codes`: A fine block's 9 codes differ; slot 0 holds 4, the block itself. Slots 0 to live_slots - 1 of a fine block are used; some fine block uses all 9. `coarse_blocks`: the 6 coarse blocks of a fine block in slab s differ and lie in slabs s - 1, s, s + 1 (mod 32); the first lies in slab s.
All inputs are finite; a program needn't handle non-finite values.
Results may differ from the reference program's by a relative error of at most 0.0029.
Values may be sent and summed in bfloat16 or wider, within the bound.
No kernel may reach another device: no remote copies, remote signals or barrier semaphores. Data moves between devices by JAX's collectives and lax.ppermute only.
A program may use at most 128 MiB of HBM per device.

```python
import jax
import jax.numpy as jnp
from jax import lax

BLK = 64
KA = 9
KP = 6
CB = 4
FX = 4
FY = 4
NXB = 64
NYB = 128
N_ROW = 16
N_COL = 32


def draw_neighbour_codes(key, part):
    first_count = N_ROW * FX
    second_count = N_COL * FY
    codes = jnp.arange(9, dtype=jnp.int32)
    scores = jax.random.randint(jax.random.fold_in(key, 5), (first_count, second_count, 9), 0, 1 << 20) * 16 + codes
    scores = jnp.where(codes == 4, -1, scores)
    ordered = jnp.argsort(scores, axis=-1)
    return ordered[..., :KA].astype(jnp.int32)


def draw_live_slots(key, part):
    first_count = N_ROW * FX
    second_count = N_COL * FY
    keys = jax.random.split(jax.random.fold_in(key, 11), 3)
    density = jax.random.randint(keys[0], (N_ROW, N_COL), 2, KA + 1)
    density = jnp.repeat(jnp.repeat(density, FX, axis=0), FY, axis=1)
    counts = 1 + jax.random.randint(keys[1], (first_count, second_count), 0, 1 << 20) % density
    chosen_spot = jax.random.randint(keys[2], (), 0, first_count * second_count)
    flat_index = jnp.arange(first_count * second_count).reshape(first_count, second_count)
    return jnp.where(flat_index == chosen_spot, KA, counts).astype(jnp.int32)


def draw_coarse_blocks(key, part):
    first_count = N_ROW * FX
    second_count = N_COL * FY
    keys = jax.random.split(jax.random.fold_in(key, 23), 2)
    aggregate = jax.random.randint(keys[0], (first_count, second_count), 0, CB)
    codes = jnp.arange(3 * CB, dtype=jnp.int32)
    scores = jax.random.randint(keys[1], (first_count, second_count, 3 * CB), 0, 1 << 18) * 4096 + codes
    scores = jnp.where(codes == CB + aggregate[..., None], -1, scores)
    chosen = jnp.argsort(scores, axis=-1)[..., :KP]
    slab_number = (jnp.arange(second_count) // FY)[None, :, None]
    return (jnp.mod(slab_number + chosen // CB - 1, N_COL) * CB + chosen % CB).astype(jnp.int32)


def block_scale(stream_key, shape, cuts, low, largest):
    loudness, own = 1.0, jax.random.fold_in(stream_key, 6)
    for dim, parts in cuts:
        heights = jnp.exp(jax.random.uniform(jax.random.fold_in(own, dim), (parts,), jnp.float32, low / len(cuts), largest / len(cuts)))
        loudness = loudness * jnp.repeat(heights, shape[dim] // parts).reshape([-1 if axis == dim else 1 for axis in range(len(shape))])
    return loudness


def normal_values(rng, extent, scale, bound, shards=(), held_as=jnp.bfloat16):
    gain = block_scale(rng, extent, shards, -0.22, 0.18) if shards else 1.0
    values = jax.random.normal(rng, extent, jnp.float32) * scale * gain
    return jnp.minimum(jnp.maximum(values, -bound), bound).astype(held_as)


def setup_inputs(seed: int = 0) -> dict:
    seeds = jax.random.split(jax.random.key(seed), 6)
    operator_tiles = normal_values(seeds[0], (NXB, NYB, KA, BLK, BLK), (KA * BLK) ** -0.5, 0.25, ((0, 16), (1, 32)))
    neighbour_codes = draw_neighbour_codes(jax.random.fold_in(seeds[5], 71), 0)
    live_slots = draw_live_slots(jax.random.fold_in(seeds[5], 71), 0)
    prolong_tiles = normal_values(seeds[3], (NXB, NYB, KP, BLK, BLK), BLK ** -0.5, 0.75, ((0, 16), (1, 32)))
    coarse_blocks = draw_coarse_blocks(jax.random.fold_in(seeds[5], 71), 0)
    return {"operator_tiles": operator_tiles, "neighbour_codes": neighbour_codes, "live_slots": live_slots, "prolong_tiles": prolong_tiles, "coarse_blocks": coarse_blocks}


def reference(operator_tiles, neighbour_codes, live_slots, prolong_tiles, coarse_blocks):
    highest = lax.Precision.HIGHEST
    window_cols = 5 * CB
    window_rows = 3 * CB
    zero_index = jnp.zeros((), jnp.int32)

    def slab_partial(slab_index):
        col_start = (slab_index * FY).astype(jnp.int32)
        second_index = col_start + jnp.arange(FY, dtype=jnp.int32)

        def row_step(running, row_block):
            op_row = lax.dynamic_slice(operator_tiles, (row_block, col_start, zero_index, zero_index, zero_index), (1, FY, KA, BLK, BLK))[0]
            codes_row = lax.dynamic_slice(neighbour_codes, (row_block, col_start, zero_index), (1, FY, KA))[0]
            live_row = lax.dynamic_slice(live_slots, (row_block, col_start), (1, FY))[0]
            own_tiles = lax.dynamic_slice(prolong_tiles, (row_block, col_start, zero_index, zero_index, zero_index), (1, FY, KP, BLK, BLK))[0]
            own_blocks = lax.dynamic_slice(coarse_blocks, (row_block, col_start, zero_index), (1, FY, KP))[0]
            near_first = jnp.mod(row_block + codes_row // 3 - 1, NXB).astype(jnp.int32)
            near_second = jnp.mod(second_index[:, None] + codes_row % 3 - 1, NYB).astype(jnp.int32)
            near_tiles = prolong_tiles[near_first, near_second].astype(jnp.float32)
            near_blocks = coarse_blocks[near_first, near_second]
            col_place = jnp.mod(near_blocks // CB - slab_index + 2, N_COL) * CB + near_blocks % CB
            col_hot = (col_place[..., None] == jnp.arange(window_cols)).astype(jnp.float32)
            live_mask = (jnp.arange(KA) < live_row[:, None]).astype(jnp.float32)
            products = jnp.einsum("mkab,mklbc->mklac", op_row.astype(jnp.float32), near_tiles, precision=highest)
            products = products * live_mask[:, :, None, None, None]
            image_panel = jnp.einsum("mklac,mklq->maqc", products, col_hot, precision=highest)
            image_panel = image_panel.reshape(FY, BLK, window_cols * BLK).astype(jnp.bfloat16)
            row_place = jnp.mod(own_blocks // CB - slab_index + 1, N_COL) * CB + own_blocks % CB
            row_hot = (row_place[..., None] == jnp.arange(window_rows)).astype(jnp.float32)
            contrib = jnp.einsum("mlba,mbc->mlac", own_tiles.astype(jnp.float32), image_panel.astype(jnp.float32), precision=highest)
            running = running + jnp.einsum("mlac,mlr->rac", contrib, row_hot, precision=highest)
            return running, None

        start_sum = jnp.zeros((window_rows, BLK, window_cols * BLK), jnp.float32)
        total, unused = lax.scan(row_step, start_sum, jnp.arange(NXB, dtype=jnp.int32))
        return total.reshape(3, CB * BLK, window_cols * BLK)

    partials = lax.map(slab_partial, jnp.arange(N_COL, dtype=jnp.int32))
    slab_rows = CB * BLK
    own_rows = partials[:, 1]
    from_next = jnp.roll(partials[:, 0], -1, axis=0)
    from_prev = jnp.roll(partials[:, 2], 1, axis=0)
    combined = jnp.pad(own_rows, ((0, 0), (0, 0), (slab_rows, slab_rows)))
    combined = combined + jnp.pad(from_next, ((0, 0), (0, 0), (2 * slab_rows, 0)))
    combined = combined + jnp.pad(from_prev, ((0, 0), (0, 0), (0, 2 * slab_rows)))
    return combined
```

```python
import jax
import jax.numpy as jnp
from jax import lax
from jax.experimental import pallas as pl
from jax.experimental.pallas import tpu as pltpu
from jax.sharding import PartitionSpec as P

CB = 4
B = 64
ROWS = 16
COLS = 32
F32 = jnp.float32
BF16 = jnp.bfloat16


def joint(rule):
    pairs = []
    for r in range(ROWS):
        for s in range(COLS):
            r2, s2 = rule(r, s)
            pairs.append((r * COLS + s, (r2 % ROWS) * COLS + s2 % COLS))
    return pairs


def send(value, rule):
    return lax.ppermute(value, ("row", "col"), joint(rule))


def sign(s):
    return 1 if s % 2 == 0 else -1


def place_kernel(core_ref, inv_ref, p_ref, po_ref, cross_ref, chip_ref, up_ref, down_ref):
    def block(b, carry):
        y = b // 4
        x = b % 4
        row = pl.multiple_of(b * B, B)

        def tile(r):
            j = inv_ref[b * 12 + r]
            value = p_ref[(x * 4 + y) * 6 + jnp.maximum(j - 1, 0)]
            return jnp.where(j > 0, value, jnp.zeros_like(value))

        for m in range(6):
            pair = jnp.concatenate([tile(2 * m), tile(2 * m + 1)], axis=1)
            po_ref[pl.ds(row, B), 128 * m : 128 * (m + 1)] = pair
        return carry

    lax.fori_loop(0, 16, block, 0)
    core = core_ref[0]
    cross_row = pl.multiple_of(core * 768, 256)
    chip_row = pl.multiple_of(768 - core * 768, 256)
    cross_ref[...] = po_ref[pl.ds(cross_row, 256), :]
    chip_ref[...] = po_ref[pl.ds(chip_row, 256), :]
    for y in range(4):
        up_ref[64 * y : 64 * y + 64, :] = po_ref[256 * y + 192 : 256 * y + 256, :]
        down_ref[64 * y : 64 * y + 64, :] = po_ref[256 * y : 256 * y + 64, :]


def smem():
    return pl.BlockSpec(memory_space=pltpu.SMEM)


def vmem():
    return pl.BlockSpec(memory_space=pltpu.VMEM)


def place(core, inv, tiles):
    edge = jax.ShapeDtypeStruct((256, 768), BF16)
    return pl.pallas_call(
        place_kernel,
        out_shape=(jax.ShapeDtypeStruct((1024, 768), BF16), edge, edge, edge, edge),
        in_specs=[smem(), smem(), vmem()],
        out_specs=(vmem(),) * 5,
        name="place",
    )(core, inv, tiles)


SLOTS = (
    ((1, 2), (None, None), (0, None)),
    ((0, 1), (2, None), (None, None)),
    ((None, 0), (1, 2), (None, None)),
    ((None, None), (0, 1), (None, 2)),
)


def reverse3(v):
    return (v & 1) * 4 + (v & 2) + (v >> 2)


def product_kernel(
    pos_ref, aidx_ref, a_ref, po_ref, cross_ref, chip_ref, up_ref, down_ref, upc_ref, downc_ref,
    keep_ref, swap_ref, same_ref, other_ref, ad_ref, pe_ref, im_ref, res_ref,
):
    core = pos_ref[0]
    r = pos_ref[1]

    def fill(b, carry):
        y = b // 4

        def tile(x, c):
            if c is None:
                return jnp.zeros((B, B), BF16)
            k = aidx_ref[(y * 4 + x) * 9 + c]
            value = a_ref[(x * 4 + y) * 9 + jnp.maximum(k, 0)]
            return jnp.where(k >= 0, value, jnp.zeros_like(value))

        for x in range(4):
            @pl.when(b % 4 == x)
            def _():
                for dy in range(3):
                    for m in range(3):
                        left, right = SLOTS[x][m]
                        left = None if left is None else left * 3 + dy
                        right = None if right is None else right * 3 + dy
                        pair = jnp.concatenate([tile(x, left), tile(x, right)], axis=1)
                        lane = 384 * dy + 128 * m
                        ad_ref[y, 64 * x : 64 * x + 64, lane : lane + 128] = pair
        return carry

    lax.fori_loop(0, 16, fill, 0)
    for y in range(4):
        pe_ref[y + 1, 0:256, :] = po_ref[256 * y : 256 * y + 256, :]
        pe_ref[y + 1, 256:320, :] = up_ref[64 * y : 64 * y + 64, :]
        pe_ref[y + 1, 320:384, :] = down_ref[64 * y : 64 * y + 64, :]
    cross_at = core * 5
    chip_at = 5 - core * 5
    pe_ref[cross_at, 0:256, :] = cross_ref[...]
    pe_ref[chip_at, 0:256, :] = chip_ref[...]
    pe_ref[cross_at, 256:320, :] = upc_ref[0:64, :]
    pe_ref[chip_at, 256:320, :] = upc_ref[64:128, :]
    pe_ref[cross_at, 320:384, :] = downc_ref[0:64, :]
    pe_ref[chip_at, 320:384, :] = downc_ref[64:128, :]

    def dot(a, b):
        return jnp.dot(a, b, preferred_element_type=F32)

    for y in range(4):
        rows = slice(256 * y, 256 * y + 256)
        if y in (1, 2):
            total = None
            for dy in range(3):
                part = dot(ad_ref[y, :, 384 * dy : 384 * dy + 384], pe_ref[y + dy])
                total = part if total is None else total + part
            im_ref[rows, 256:1024] = total.astype(BF16)
        else:
            edge_dy = 0 if y == 0 else 2
            edge = dot(ad_ref[y, :, 384 * edge_dy : 384 * edge_dy + 384], pe_ref[y + edge_dy])
            first, second = (1, 2) if y == 0 else (0, 1)
            total = dot(ad_ref[y, :, 384 * first : 384 * first + 384], pe_ref[y + first])
            total = total + dot(ad_ref[y, :, 384 * second : 384 * second + 384], pe_ref[y + second])
            if y == 0:
                im_ref[rows, 0:256] = edge[:, 0:256].astype(BF16)
                im_ref[rows, 256:768] = (edge[:, 256:768] + total[:, 0:512]).astype(BF16)
                im_ref[rows, 768:1024] = total[:, 512:768].astype(BF16)
            else:
                im_ref[rows, 256:512] = total[:, 0:256].astype(BF16)
                im_ref[rows, 512:1024] = (edge[:, 0:512] + total[:, 256:768]).astype(BF16)
                im_ref[rows, 1024:1280] = edge[:, 512:768].astype(BF16)

    def piece(window, kind, store):
        lanes = pl.ds(pl.multiple_of(window * 256, 256), 256)
        for chunk in range(5):
            rows = slice(0, 256) if chunk == 0 else slice(768, 1024) if chunk == 4 else slice(0, 1024)
            cols = slice(256 * chunk, 256 * chunk + 256)
            out = lax.dot_general(
                po_ref[rows, lanes], im_ref[rows, cols], (((0,), (0,)), ((), ())),
                preferred_element_type=F32,
            )
            for o in range(16):
                shifted = (o - r - kind + 32) % 16
                flow = shifted // 8
                near = jnp.where(flow == 0, shifted, 15 - shifted)
                half = (flow + core) % 2
                row = pl.multiple_of((half * 8 + reverse3(near)) * 16, 16)
                res_ref[pl.ds(row, 16), :] = out[16 * o : 16 * o + 16, :]
            store(cols)

    def store_outer(cols):
        same_ref[:, cols] = res_ref[0:128, :].astype(BF16)
        other_ref[:, cols] = res_ref[128:256, :].astype(BF16)

    def store_own(cols):
        keep_ref[0:128, cols] = res_ref[0:128, :]
        swap_ref[0:128, cols] = res_ref[128:256, :].astype(BF16)

    def store_partner(cols):
        keep_ref[128:256, cols] = res_ref[0:128, :]
        swap_ref[128:256, cols] = res_ref[128:256, :].astype(BF16)

    piece(core * 2, 1 - core, store_outer)
    piece(1 + core * 0, core, store_own)
    piece(2 - core * 2, 1 - core, store_partner)


def products(pos, aidx, a, po, cross, chip, up, down, upc, downc):
    half = jax.ShapeDtypeStruct((128, 1280), BF16)
    return pl.pallas_call(
        product_kernel,
        out_shape=(
            jax.ShapeDtypeStruct((256, 1280), F32),
            jax.ShapeDtypeStruct((256, 1280), BF16),
            half,
            half,
        ),
        in_specs=[smem(), smem()] + [vmem()] * 8,
        out_specs=(vmem(),) * 4,
        scratch_shapes=[
            pltpu.VMEM((4, 256, 1152), BF16),
            pltpu.VMEM((6, 384, 768), BF16),
            pltpu.VMEM((1024, 1280), BF16),
            pltpu.VMEM((256, 256), F32),
        ],
        name="products",
    )(pos, aidx, a, po, cross, chip, up, down, upc, downc)


def merge_kernel(pos_ref, keep_ref, swap_ref, same_ref, other_ref, acc_ref, msg_ref, sum_ref):
    def merge(low, high):
        sum_ref[...] = jnp.zeros_like(sum_ref)
        sum_ref[0, :, 256:1536] = keep_ref[0:128, :]
        sum_ref[0, :, high : high + 1280] += swap_ref[128:256, :].astype(F32)
        sum_ref[0, :, low : low + 1280] += other_ref[...].astype(F32)
        sum_ref[1, :, low : low + 1280] = keep_ref[128:256, :]
        sum_ref[1, :, 256:1536] += swap_ref[0:128, :].astype(F32)
        sum_ref[1, :, high : high + 1280] += same_ref[...].astype(F32)

    @pl.when(pos_ref[0] == 0)
    def _():
        merge(0, 512)

    @pl.when(pos_ref[0] == 1)
    def _():
        merge(512, 0)

    acc_ref[...] = sum_ref[:, 0:64, :]
    msg_ref[...] = sum_ref[:, 64:128, :].astype(BF16)


def merged(pos, keep, swap, same, other):
    return pl.pallas_call(
        merge_kernel,
        out_shape=(
            jax.ShapeDtypeStruct((2, 64, 1792), F32),
            jax.ShapeDtypeStruct((2, 64, 1792), BF16),
        ),
        in_specs=[smem()] + [vmem()] * 4,
        out_specs=(vmem(), vmem()),
        scratch_shapes=[pltpu.VMEM((2, 128, 1792), F32)],
        name="merge",
    )(pos, keep, swap, same, other)


def per_device(operator_tiles, neighbour_codes, live_slots, prolong_tiles, coarse_blocks):
    r = lax.axis_index("row")
    s = lax.axis_index("col")
    core = s % 2
    pos = jnp.stack([core, r]).astype(jnp.int32)

    place_of = jnp.mod(coarse_blocks // CB - s + 1, COLS) * CB + coarse_blocks % CB
    hit = place_of[..., None] == jnp.arange(12)
    number = jnp.arange(1, 7, dtype=jnp.int32)[:, None]
    inv = jnp.sum(jnp.where(hit, number, 0), axis=2).transpose(1, 0, 2).reshape(-1)
    code_hit = neighbour_codes[..., None] == jnp.arange(9)
    slot = jnp.sum(jnp.where(code_hit, jnp.arange(9, dtype=jnp.int32)[:, None], 0), axis=2)
    slot = jnp.where(slot < live_slots[..., None], slot, -1)
    aidx = slot.transpose(1, 0, 2).reshape(-1)

    po, cross, chip, up, down = place(pos, inv, prolong_tiles.reshape(96, B, B))
    up_in = send(up, lambda r, s: (r + 1, s))
    down_in = send(down, lambda r, s: (r - 1, s))
    cross_in = send(cross, lambda r, s: (r, s - sign(s)))
    chip_in = send(chip, lambda r, s: (r, s + sign(s)))
    upc = jnp.concatenate([cross_in[192:256], chip_in[192:256]], axis=0)
    downc = jnp.concatenate([cross_in[0:64], chip_in[0:64]], axis=0)
    upc_in = send(upc, lambda r, s: (r + 1, s))
    downc_in = send(downc, lambda r, s: (r - 1, s))

    keep, swap, same, other = products(
        pos, aidx, operator_tiles.reshape(144, B, B), po,
        cross_in, chip_in, up_in, down_in, upc_in, downc_in,
    )
    other_in = send(other, lambda r, s: (r, s - sign(s)))
    same_in = send(same, lambda r, s: (r, s - 2 * sign(s)))
    swap_in = send(swap, lambda r, s: (r, s + sign(s)))
    acc, msg = merged(pos, keep, swap_in, same_in, other_in)
    for step, size in ((1, 32), (2, 16)):
        got = send(msg, lambda r, s: (r + step * sign(s), s)).astype(F32)
        msg = (acc[:, size:] + got[:, size:]).astype(BF16)
        acc = acc[:, :size] + got[:, :size]
    acc = acc + send(msg, lambda r, s: (r + 4 * sign(s), s)).astype(F32)
    last = send(acc[1], lambda r, s: (r + sign(s), s + sign(s)))
    return (acc[0] + last)[None]


def solution(mesh):
    in_specs = (
        P("row", "col", None, None, None),
        P("row", "col", None),
        P("row", "col"),
        P("row", "col", None, None, None),
        P("row", "col", None),
    )
    out_specs = P("col", "row", None)
    return jax.shard_map(
        per_device, mesh=mesh, in_specs=in_specs, out_specs=out_specs, check_vma=False
    )
```

```python
import jax
import jax.numpy as jnp
from jax import lax
from jax.experimental import pallas as pl
from jax.experimental.pallas import tpu as pltpu
from jax.sharding import PartitionSpec as P


CB = 4
B = 64
ROWS = 16
COLS = 32
F32 = jnp.float32
BF16 = jnp.bfloat16


def joint(rule):
    pairs = []
    for r in range(ROWS):
        for s in range(COLS):
            r2, s2 = rule(r, s)
            pairs.append((r * COLS + s, (r2 % ROWS) * COLS + s2 % COLS))
    return pairs


def send(value, rule):
    return lax.ppermute(value, ("row", "col"), joint(rule))


def sign(s):
    return 1 if s % 2 == 0 else -1


def place_kernel(core_ref, inv_ref, p_ref, po_ref, cross_ref, chip_ref, up_ref, down_ref):
    def block(b, carry):
        y = b // 4
        x = b % 4
        row = pl.multiple_of(b * B, B)

        def tile(r):
            j = inv_ref[b * 12 + r]
            value = p_ref[(x * 4 + y) * 6 + jnp.maximum(j - 1, 0)]
            return jnp.where(j > 0, value, jnp.zeros_like(value))

        for m in range(6):
            pair = jnp.concatenate([tile(2 * m), tile(2 * m + 1)], axis=1)
            po_ref[pl.ds(row, B), 128 * m : 128 * (m + 1)] = pair
        return carry

    lax.fori_loop(0, 16, block, 0)
    core = core_ref[0]
    cross_row = pl.multiple_of(core * 768, 256)
    chip_row = pl.multiple_of(768 - core * 768, 256)
    cross_ref[...] = po_ref[pl.ds(cross_row, 256), :]
    chip_ref[...] = po_ref[pl.ds(chip_row, 256), :]
    for y in range(4):
        up_ref[64 * y : 64 * y + 64, :] = po_ref[256 * y + 192 : 256 * y + 256, :]
        down_ref[64 * y : 64 * y + 64, :] = po_ref[256 * y : 256 * y + 64, :]


def smem():
    return pl.BlockSpec(memory_space=pltpu.SMEM)


def vmem():
    return pl.BlockSpec(memory_space=pltpu.VMEM)


def budget(mib, flops, moved):
    return dict(
        compiler_params=pltpu.CompilerParams(vmem_limit_bytes=mib << 20),
        cost_estimate=pl.CostEstimate(flops=flops, bytes_accessed=moved, transcendentals=0),
    )


def place(core, inv, tiles):
    edge = jax.ShapeDtypeStruct((256, 768), BF16)
    return pl.pallas_call(
        place_kernel,
        out_shape=(jax.ShapeDtypeStruct((1024, 768), BF16), edge, edge, edge, edge),
        in_specs=[smem(), smem(), vmem()],
        out_specs=(vmem(),) * 5,
        name="place",
        **budget(6, 0, 6000000),
    )(core, inv, tiles)


SLOTS = (
    ((1, 2), (None, None), (0, None)),
    ((0, 1), (2, None), (None, None)),
    ((None, 0), (1, 2), (None, None)),
    ((None, None), (0, 1), (None, 2)),
)


def dot(a, b):
    return jnp.dot(a, b, preferred_element_type=F32)


def local_kernel(pos_ref, aidx_ref, a_ref, po_ref, ad_ref, outer_ref, rest_ref, im_ref):
    core = pos_ref[0]
    r = pos_ref[1]

    def fill(b, carry):
        y = b // 4

        def tile(x, c):
            if c is None:
                return jnp.zeros((B, B), BF16)
            k = aidx_ref[(y * 4 + x) * 9 + c]
            value = a_ref[(x * 4 + y) * 9 + jnp.maximum(k, 0)]
            return jnp.where(k >= 0, value, jnp.zeros_like(value))

        for x in range(4):
            @pl.when(b % 4 == x)
            def _():
                for dy in range(3):
                    for m in range(3):
                        left, right = SLOTS[x][m]
                        left = None if left is None else left * 3 + dy
                        right = None if right is None else right * 3 + dy
                        pair = jnp.concatenate([tile(x, left), tile(x, right)], axis=1)
                        lane = 256 * dy + 128 * m if m < 2 else 768 + 128 * dy
                        ad_ref[y, 64 * x : 64 * x + 64, lane : lane + 128] = pair
        return carry

    lax.fori_loop(0, 16, fill, 0)

    for y in range(4):
        first = 1 if y == 0 else 0
        last = 1 if y == 3 else 2
        im_ref[256 * y : 256 * y + 256, :] = dot(
            ad_ref[y, :, 256 * first : 256 * last + 256],
            po_ref[256 * (y + first - 1) : 256 * (y + last), :],
        )

    windows = ((core * 2, 1 - core), (1 + core * 0, core), (2 - core * 2, 1 - core))
    for n, (window, kind) in enumerate(windows):
        lanes = pl.ds(pl.multiple_of(window * 256, 256), 256)
        for y in range(4):
            flipped = po_ref[256 * y : 256 * y + 256, lanes].T
            for o in range(16):
                shifted = (o - r - kind + 32) % 16
                flow = shifted // 8
                near = jnp.where(flow == 0, shifted, 15 - shifted)
                half = (flow + core) % 2
                spot = half * 8 + (near % 4) * 2 + near // 4
                row = pl.multiple_of(max(n - 1, 0) * 256 + spot * 16, 16)
                pt_ref = rest_ref if n else outer_ref
                pt_ref[pl.ds(row, 16), 256 * y : 256 * y + 256] = flipped[16 * o : 16 * o + 16, :]


def local_products(pos, aidx, a, po):
    return pl.pallas_call(
        local_kernel,
        out_shape=(
            jax.ShapeDtypeStruct((4, 256, 1152), BF16),
            jax.ShapeDtypeStruct((256, 1024), BF16),
            jax.ShapeDtypeStruct((512, 1024), BF16),
            jax.ShapeDtypeStruct((1024, 768), F32),
        ),
        in_specs=[smem(), smem(), vmem(), vmem()],
        out_specs=(vmem(),) * 4,
        name="local_products",
        **budget(12, 1000000000, 12000000),
    )(pos, aidx, a, po)


def pieces(pt_ref, base, im_ref, store):
    for chunk in range(5):
        k = slice(0, 256) if chunk == 0 else slice(768, 1024) if chunk == 4 else slice(0, 1024)
        cols = slice(256 * chunk, 256 * chunk + 256)
        store(cols, dot(pt_ref[base : base + 256, k], im_ref[k, cols]))


def halo_kernel(
    pos_ref, ad_ref, pt_ref, part_ref, cross_ref, chip_ref, up_ref, down_ref, upc_ref, downc_ref,
    im_ref, same_ref, other_ref, side_ref, hr_ref,
):
    core = pos_ref[0]
    for y in range(4):
        hr_ref[y + 1, 0:64, :] = up_ref[64 * y : 64 * y + 64, :]
        hr_ref[y + 1, 64:128, :] = down_ref[64 * y : 64 * y + 64, :]
    side_ref[core] = cross_ref[...]
    side_ref[1 - core] = chip_ref[...]
    hr_ref[core * 5, 0:64, :] = upc_ref[0:64, :]
    hr_ref[core * 5, 64:128, :] = downc_ref[0:64, :]
    hr_ref[5 - core * 5, 0:64, :] = upc_ref[64:128, :]
    hr_ref[5 - core * 5, 64:128, :] = downc_ref[64:128, :]

    for y in range(4):
        rows = slice(256 * y, 256 * y + 256)
        first = 1 if y == 0 else 0
        last = 1 if y == 3 else 2
        count = last - first + 1
        total = part_ref[rows, :] + dot(
            ad_ref[y, :, 768 + 128 * first : 896 + 128 * last],
            hr_ref[y + first : y + last + 1].reshape(128 * count, 768),
        )
        if count == 3:
            im_ref[rows, 256:1024] = total.astype(BF16)
            continue
        dy, side, at = (0, 0, 0) if y == 0 else (2, 1, 5)
        edge = dot(ad_ref[y, :, 256 * dy : 256 * dy + 256], side_ref[side])
        edge = edge + dot(ad_ref[y, :, 768 + 128 * dy : 896 + 128 * dy], hr_ref[at])
        if y == 0:
            im_ref[rows, 0:256] = edge[:, 0:256].astype(BF16)
            im_ref[rows, 256:768] = (edge[:, 256:768] + total[:, 0:512]).astype(BF16)
            im_ref[rows, 768:1024] = total[:, 512:768].astype(BF16)
        else:
            im_ref[rows, 256:512] = total[:, 0:256].astype(BF16)
            im_ref[rows, 512:1024] = (edge[:, 0:512] + total[:, 256:768]).astype(BF16)
            im_ref[rows, 1024:1280] = edge[:, 512:768].astype(BF16)

    def store(cols, out):
        same_ref[:, cols] = out[0:128].astype(BF16)
        other_ref[:, cols] = out[128:256].astype(BF16)

    pieces(pt_ref, 0, im_ref, store)


def halo_products(pos, ad, pt, part, *halo):
    half = jax.ShapeDtypeStruct((128, 1280), BF16)
    return pl.pallas_call(
        halo_kernel,
        out_shape=(jax.ShapeDtypeStruct((1024, 1280), BF16), half, half),
        in_specs=[smem()] + [vmem()] * 9,
        out_specs=(vmem(),) * 3,
        scratch_shapes=[pltpu.VMEM((2, 256, 768), BF16), pltpu.VMEM((6, 128, 768), BF16)],
        name="halo_products",
        **budget(12, 1500000000, 12000000),
    )(pos, ad, pt, part, *halo)


def own_kernel(pt_ref, im_ref, keep_ref, swap_ref):
    for n in range(2):
        def store(cols, out):
            keep_ref[128 * n : 128 * n + 128, cols] = out[0:128]
            swap_ref[128 * n : 128 * n + 128, cols] = out[128:256].astype(BF16)

        pieces(pt_ref, 256 * n, im_ref, store)


def own_pieces(pt, im):
    return pl.pallas_call(
        own_kernel,
        out_shape=(
            jax.ShapeDtypeStruct((256, 1280), F32),
            jax.ShapeDtypeStruct((256, 1280), BF16),
        ),
        in_specs=[vmem(), vmem()],
        out_specs=(vmem(), vmem()),
        name="own_pieces",
        **budget(8, 1400000000, 6000000),
    )(pt, im)


def merge_kernel(
    pos_ref, keep_own, keep_partner, swap_own, swap_partner, same_ref, other_ref, out_ref, sum_ref
):
    def merge(low, high):
        def add(n, at, ref):
            sum_ref[n, :, at : at + 1280] += ref[...].astype(F32)

        zero = jnp.zeros((32, 256), F32)
        for n in range(2):
            for at in (0, 256, 1280, 1536):
                sum_ref[n, :, at : at + 256] = zero
        sum_ref[0, :, 256:1536] = keep_own[...]
        sum_ref[1, :, 256:1536] = swap_own[...].astype(F32)
        add(0, high, swap_partner)
        add(0, low, other_ref)
        add(1, low, keep_partner)
        add(1, high, same_ref)

    @pl.when(pos_ref[0] == 0)
    def _():
        merge(0, 512)

    @pl.when(pos_ref[0] == 1)
    def _():
        merge(512, 0)

    out_ref[...] = sum_ref[...].astype(out_ref.dtype)


def merged(pos, keep, swap, same, other, group):
    def rows(at):
        return pl.BlockSpec((32, 1280), lambda i: (at, 0))

    return pl.pallas_call(
        merge_kernel,
        grid=(1,),
        out_shape=jax.ShapeDtypeStruct((2, 32, 1792), F32 if group == 0 else BF16),
        in_specs=[smem()] + [rows(group), rows(group + 4)] * 2 + [rows(group)] * 2,
        out_specs=pl.BlockSpec((2, 32, 1792), lambda i: (0, 0, 0)),
        scratch_shapes=[pltpu.VMEM((2, 32, 1792), F32)],
        **budget(4, 0, 1000000),
    )(pos, keep, keep, swap, swap, same, other)


def body(operator_tiles, neighbour_codes, live_slots, prolong_tiles, coarse_blocks):
    r = lax.axis_index("row")
    s = lax.axis_index("col")
    core = s % 2
    pos = jnp.stack([core, r]).astype(jnp.int32)

    place_of = jnp.mod(coarse_blocks // CB - s + 1, COLS) * CB + coarse_blocks % CB
    hit = place_of[..., None] == jnp.arange(12)
    number = jnp.arange(1, 7, dtype=jnp.int32)[:, None]
    inv = jnp.sum(jnp.where(hit, number, 0), axis=2).transpose(1, 0, 2).reshape(-1)
    code_hit = neighbour_codes[..., None] == jnp.arange(9)
    slot = jnp.sum(jnp.where(code_hit, jnp.arange(9, dtype=jnp.int32)[:, None], 0), axis=2)
    slot = jnp.where(slot < live_slots[..., None], slot, -1)
    aidx = slot.transpose(1, 0, 2).reshape(-1)

    po, cross, chip, up, down = place(pos, inv, prolong_tiles.reshape(96, B, B))
    cross_in = send(cross, lambda r, s: (r, s - sign(s)))
    chip_in = send(chip, lambda r, s: (r, s + sign(s)))
    up_in = send(up, lambda r, s: (r + 1, s))
    down_in = send(down, lambda r, s: (r - 1, s))
    upc = jnp.concatenate([cross_in[192:256], chip_in[192:256]], axis=0)
    downc = jnp.concatenate([cross_in[0:64], chip_in[0:64]], axis=0)
    upc_in = send(upc, lambda r, s: (r + 1, s))
    downc_in = send(downc, lambda r, s: (r - 1, s))

    ad, outer, rest, part = local_products(pos, aidx, operator_tiles.reshape(144, B, B), po)
    im, same, other = halo_products(
        pos, ad, outer, part, cross_in, chip_in, up_in, down_in, upc_in, downc_in
    )
    other_in = send(other, lambda r, s: (r, s - sign(s)))
    same_in = send(same, lambda r, s: (r, s - 2 * sign(s)))
    keep, swap = own_pieces(rest, im)
    swap_in = send(swap, lambda r, s: (r, s + sign(s)))
    moved = {}
    for step in (3, 2, 1):
        msg = merged(pos, keep, swap_in, same_in, other_in, step)
        moved[step] = send(msg, lambda r, s: (r + step * sign(s), s))
    acc = merged(pos, keep, swap_in, same_in, other_in, 0)
    for step in (1, 2, 3):
        acc = acc + moved[step].astype(F32)
    msg = acc[:, 16:].astype(BF16)
    acc = acc[:, :16] + send(msg, lambda r, s: (r + 4 * sign(s), s)).astype(F32)
    last = send(acc[1], lambda r, s: (r + sign(s), s + sign(s)))
    return (acc[0] + last)[None]


def solution(mesh):
    in_specs = (
        P("row", "col", None, None, None),
        P("row", "col", None),
        P("row", "col"),
        P("row", "col", None, None, None),
        P("row", "col", None),
    )
    out_specs = P("col", "row", None)
    return jax.shard_map(body, mesh=mesh, in_specs=in_specs, out_specs=out_specs, check_vma=False)
```

```python
import jax
import jax.numpy as jnp
from jax import lax
from jax.experimental import pallas as pl
from jax.experimental.pallas import tpu as pltpu
from jax.sharding import PartitionSpec as P


B = 64
ROWS = 16
COLS = 32
F32 = jnp.float32
BF16 = jnp.bfloat16


def joint(rule):
    pairs = []
    for r in range(ROWS):
        for s in range(COLS):
            r2, s2 = rule(r, s)
            pairs.append((r * COLS + s, (r2 % ROWS) * COLS + s2 % COLS))
    return pairs


def send(value, rule):
    return lax.ppermute(value, ("row", "col"), joint(rule))


def sign(s):
    return 1 if s % 2 == 0 else -1


def smem():
    return pl.BlockSpec(memory_space=pltpu.SMEM)


def vmem():
    return pl.BlockSpec(memory_space=pltpu.VMEM)


def budget(mib, flops, moved):
    return dict(
        compiler_params=pltpu.CompilerParams(vmem_limit_bytes=mib << 20),
        cost_estimate=pl.CostEstimate(flops=flops, bytes_accessed=moved, transcendentals=0),
    )


def place_blocks(ys, pos_ref, blocks_ref, p_ref, po_refs, buf_ref, inv_ref, sems):
    spots = [(n, y, x) for n, y in enumerate(ys) for x in range(4)]
    copies = [
        pltpu.make_async_copy(p_ref.at[x, y], buf_ref.at[i], sems.at[i])
        for i, (_, y, x) in enumerate(spots)
    ]
    for copy in copies:
        copy.start()
    slab = pos_ref[2]
    for i, (_, y, x) in enumerate(spots):
        for column in range(12):
            inv_ref[i * 12 + column] = 0
        for j in range(6):
            g = blocks_ref[x, y, j]
            inv_ref[i * 12 + ((g // 4 - slab + 33) % 32) * 4 + g % 4] = j + 1
    for i, (n, _, x) in enumerate(spots):
        copies[i].wait()

        def tile(column):
            j = inv_ref[i * 12 + column]
            value = buf_ref[i, jnp.maximum(j - 1, 0)]
            return jnp.where(j > 0, value, jnp.zeros_like(value))

        for m in range(6):
            pair = jnp.concatenate([tile(2 * m), tile(2 * m + 1)], axis=1)
            po_refs[n][64 * x : 64 * x + 64, 128 * m : 128 * m + 128] = pair


def edge_kernel(pos_ref, blocks_ref, p_ref, low_ref, high_ref, cross_ref, chip_ref, *scratch):
    place_blocks((0, 3), pos_ref, blocks_ref, p_ref, (low_ref, high_ref), *scratch)

    @pl.when(pos_ref[0] == 0)
    def _():
        cross_ref[...] = low_ref[...]
        chip_ref[...] = high_ref[...]

    @pl.when(pos_ref[0] == 1)
    def _():
        cross_ref[...] = high_ref[...]
        chip_ref[...] = low_ref[...]


def middle_kernel(pos_ref, blocks_ref, p_ref, one_ref, two_ref, *scratch):
    place_blocks((1, 2), pos_ref, blocks_ref, p_ref, (one_ref, two_ref), *scratch)


def place(kernel, count, pos, blocks, tiles):
    return pl.pallas_call(
        kernel,
        out_shape=(jax.ShapeDtypeStruct((256, 768), BF16),) * count,
        in_specs=[smem(), smem(), pl.BlockSpec(memory_space=pltpu.HBM)],
        out_specs=(vmem(),) * count,
        scratch_shapes=[
            pltpu.VMEM((8, 6, B, B), BF16),
            pltpu.SMEM((96,), jnp.int32),
            pltpu.SemaphoreType.DMA((8,)),
        ],
        **budget(6, 0, 2000000),
    )(pos, blocks, tiles)


def rim_kernel(p0, p1, p2, p3, cross_ref, chip_ref, up_ref, down_ref):
    for n, ref in enumerate((p0, p1, p2, p3, cross_ref, chip_ref)):
        up_ref[64 * n : 64 * n + 64, :] = ref[192:256, :]
        down_ref[64 * n : 64 * n + 64, :] = ref[0:64, :]


def rims(*parts):
    return pl.pallas_call(
        rim_kernel,
        out_shape=(jax.ShapeDtypeStruct((384, 768), BF16),) * 2,
        in_specs=[vmem()] * 6,
        out_specs=(vmem(),) * 2,
        name="rims",
        **budget(4, 0, 2000000),
    )(*parts)


SLOTS = (
    ((1, 2), (None, None), (0, None)),
    ((0, 1), (2, None), (None, None)),
    ((None, 0), (1, 2), (None, None)),
    ((None, None), (0, 1), (None, 2)),
)


def dot(a, b):
    return jnp.dot(a, b, preferred_element_type=F32)


def local_kernel(
    pos_ref, codes_ref, live_ref, a_ref, p0, p1, p2, p3,
    ad_ref, outer_ref, rest_ref, im_ref, po_ref, aidx_ref,
):
    core = pos_ref[0]
    r = pos_ref[1]

    for y, part in enumerate((p0, p1, p2, p3)):
        po_ref[256 * y : 256 * y + 256, :] = part[...]

    def fill(b, carry):
        y = b // 4
        at = b % 4
        for k in range(9):
            aidx_ref[codes_ref[at, y, k]] = jnp.where(k < live_ref[at, y], k, -1)

        def tile(x, c):
            if c is None:
                return jnp.zeros((B, B), BF16)
            k = aidx_ref[c]
            value = a_ref[(x * 4 + y) * 9 + jnp.maximum(k, 0)]
            return jnp.where(k >= 0, value, jnp.zeros_like(value))

        for x in range(4):
            @pl.when(at == x)
            def _():
                for dy in range(3):
                    for m in range(3):
                        left, right = SLOTS[x][m]
                        left = None if left is None else left * 3 + dy
                        right = None if right is None else right * 3 + dy
                        pair = jnp.concatenate([tile(x, left), tile(x, right)], axis=1)
                        lane = 256 * dy + 128 * m if m < 2 else 768 + 128 * dy
                        ad_ref[y, 64 * x : 64 * x + 64, lane : lane + 128] = pair
        return carry

    lax.fori_loop(0, 16, fill, 0)

    for y in range(4):
        first = 1 if y == 0 else 0
        last = 1 if y == 3 else 2
        im_ref[256 * y : 256 * y + 256, :] = dot(
            ad_ref[y, :, 256 * first : 256 * last + 256],
            po_ref[256 * (y + first - 1) : 256 * (y + last), :],
        )

    windows = ((core * 2, 1 - core), (1 + core * 0, core), (2 - core * 2, 1 - core))
    for n, (window, kind) in enumerate(windows):
        lanes = pl.ds(pl.multiple_of(window * 256, 256), 256)
        for y in range(4):
            flipped = po_ref[256 * y : 256 * y + 256, lanes].T
            for o in range(16):
                shifted = (o - r - kind + 32) % 16
                flow = shifted // 8
                near = jnp.where(flow == 0, shifted, 15 - shifted)
                half = (flow + core) % 2
                spot = half * 8 + (near % 4) * 2 + near // 4
                row = pl.multiple_of(max(n - 1, 0) * 256 + spot * 16, 16)
                pt_ref = rest_ref if n else outer_ref
                pt_ref[pl.ds(row, 16), 256 * y : 256 * y + 256] = flipped[16 * o : 16 * o + 16, :]


def local_products(pos, codes, live, a, *parts):
    return pl.pallas_call(
        local_kernel,
        out_shape=(
            jax.ShapeDtypeStruct((4, 256, 1152), BF16),
            jax.ShapeDtypeStruct((256, 1024), BF16),
            jax.ShapeDtypeStruct((512, 1024), BF16),
            jax.ShapeDtypeStruct((1024, 768), F32),
        ),
        in_specs=[smem(), smem(), smem()] + [vmem()] * 5,
        out_specs=(vmem(),) * 4,
        scratch_shapes=[pltpu.VMEM((1024, 768), BF16), pltpu.SMEM((9,), jnp.int32)],
        name="local_products",
        **budget(12, 1000000000, 12000000),
    )(pos, codes, live, a, *parts)


def pieces(pt_ref, base, im_ref, store):
    for chunk in range(5):
        k = slice(0, 256) if chunk == 0 else slice(768, 1024) if chunk == 4 else slice(0, 1024)
        cols = slice(256 * chunk, 256 * chunk + 256)
        store(cols, dot(pt_ref[base : base + 256, k], im_ref[k, cols]))


def halo_kernel(
    pos_ref, ad_ref, pt_ref, part_ref, cross_ref, chip_ref, up_ref, down_ref,
    im_ref, same_ref, other_ref, side_ref, hr_ref,
):
    core = pos_ref[0]
    for y in range(4):
        hr_ref[y + 1, 0:64, :] = up_ref[64 * y : 64 * y + 64, :]
        hr_ref[y + 1, 64:128, :] = down_ref[64 * y : 64 * y + 64, :]
    side_ref[core] = cross_ref[...]
    side_ref[1 - core] = chip_ref[...]
    hr_ref[core * 5, 0:64, :] = up_ref[256:320, :]
    hr_ref[core * 5, 64:128, :] = down_ref[256:320, :]
    hr_ref[5 - core * 5, 0:64, :] = up_ref[320:384, :]
    hr_ref[5 - core * 5, 64:128, :] = down_ref[320:384, :]

    for y in range(4):
        rows = slice(256 * y, 256 * y + 256)
        first = 1 if y == 0 else 0
        last = 1 if y == 3 else 2
        count = last - first + 1
        total = part_ref[rows, :] + dot(
            ad_ref[y, :, 768 + 128 * first : 896 + 128 * last],
            hr_ref[y + first : y + last + 1].reshape(128 * count, 768),
        )
        if count == 3:
            im_ref[rows, 256:1024] = total.astype(BF16)
            continue
        dy, side, at = (0, 0, 0) if y == 0 else (2, 1, 5)
        edge = dot(ad_ref[y, :, 256 * dy : 256 * dy + 256], side_ref[side])
        edge = edge + dot(ad_ref[y, :, 768 + 128 * dy : 896 + 128 * dy], hr_ref[at])
        if y == 0:
            im_ref[rows, 0:256] = edge[:, 0:256].astype(BF16)
            im_ref[rows, 256:768] = (edge[:, 256:768] + total[:, 0:512]).astype(BF16)
            im_ref[rows, 768:1024] = total[:, 512:768].astype(BF16)
        else:
            im_ref[rows, 256:512] = total[:, 0:256].astype(BF16)
            im_ref[rows, 512:1024] = (edge[:, 0:512] + total[:, 256:768]).astype(BF16)
            im_ref[rows, 1024:1280] = edge[:, 512:768].astype(BF16)

    def store(cols, out):
        same_ref[:, cols] = out[0:128].astype(BF16)
        other_ref[:, cols] = out[128:256].astype(BF16)

    pieces(pt_ref, 0, im_ref, store)


def halo_products(pos, ad, pt, part, *halo):
    half = jax.ShapeDtypeStruct((128, 1280), BF16)
    return pl.pallas_call(
        halo_kernel,
        out_shape=(jax.ShapeDtypeStruct((1024, 1280), BF16), half, half),
        in_specs=[smem()] + [vmem()] * 7,
        out_specs=(vmem(),) * 3,
        scratch_shapes=[pltpu.VMEM((2, 256, 768), BF16), pltpu.VMEM((6, 128, 768), BF16)],
        name="halo_products",
        **budget(12, 1500000000, 12000000),
    )(pos, ad, pt, part, *halo)


def own_kernel(pt_ref, im_ref, keep_ref, swap_ref):
    for n in range(2):
        def store(cols, out):
            keep_ref[128 * n : 128 * n + 128, cols] = out[0:128]
            swap_ref[128 * n : 128 * n + 128, cols] = out[128:256].astype(BF16)

        pieces(pt_ref, 256 * n, im_ref, store)


def own_pieces(pt, im):
    return pl.pallas_call(
        own_kernel,
        out_shape=(
            jax.ShapeDtypeStruct((256, 1280), F32),
            jax.ShapeDtypeStruct((256, 1280), BF16),
        ),
        in_specs=[vmem(), vmem()],
        out_specs=(vmem(), vmem()),
        name="own_pieces",
        **budget(8, 1400000000, 6000000),
    )(pt, im)


def merge_kernel(
    pos_ref, keep_own, keep_partner, swap_own, swap_partner, same_ref, other_ref, out_ref, sum_ref
):
    def merge(low, high):
        def add(n, at, ref):
            sum_ref[n, :, at : at + 1280] += ref[...].astype(F32)

        zero = jnp.zeros((32, 256), F32)
        for n in range(2):
            for at in (0, 256, 1280, 1536):
                sum_ref[n, :, at : at + 256] = zero
        sum_ref[0, :, 256:1536] = keep_own[...]
        sum_ref[1, :, 256:1536] = swap_own[...].astype(F32)
        add(0, high, swap_partner)
        add(0, low, other_ref)
        add(1, low, keep_partner)
        add(1, high, same_ref)

    @pl.when(pos_ref[0] == 0)
    def _():
        merge(0, 512)

    @pl.when(pos_ref[0] == 1)
    def _():
        merge(512, 0)

    out_ref[...] = sum_ref[...].astype(out_ref.dtype)


def merged(pos, keep, swap, same, other, group):
    def rows(at):
        return pl.BlockSpec((32, 1280), lambda i: (at, 0))

    return pl.pallas_call(
        merge_kernel,
        grid=(1,),
        out_shape=jax.ShapeDtypeStruct((2, 32, 1792), F32 if group == 0 else BF16),
        in_specs=[smem()] + [rows(group), rows(group + 4)] * 2 + [rows(group)] * 2,
        out_specs=pl.BlockSpec((2, 32, 1792), lambda i: (0, 0, 0)),
        scratch_shapes=[pltpu.VMEM((2, 32, 1792), F32)],
        **budget(4, 0, 1000000),
    )(pos, keep, keep, swap, swap, same, other)


def body(operator_tiles, neighbour_codes, live_slots, prolong_tiles, coarse_blocks):
    r = lax.axis_index("row")
    s = lax.axis_index("col")
    core = s % 2
    pos = jnp.stack([core, r, s]).astype(jnp.int32)

    low, high, cross, chip = place(edge_kernel, 4, pos, coarse_blocks, prolong_tiles)
    cross_in = send(cross, lambda r, s: (r, s - sign(s)))
    chip_in = send(chip, lambda r, s: (r, s + sign(s)))
    one, two = place(middle_kernel, 2, pos, coarse_blocks, prolong_tiles)
    parts = (low, one, two, high)
    up, down = rims(*parts, cross_in, chip_in)
    up_in = send(up, lambda r, s: (r + 1, s))
    down_in = send(down, lambda r, s: (r - 1, s))
    ad, outer, rest, part = local_products(
        pos, neighbour_codes, live_slots, operator_tiles.reshape(144, B, B), *parts
    )
    im, same, other = halo_products(
        pos, ad, outer, part, cross_in, chip_in, up_in, down_in
    )
    other_in = send(other, lambda r, s: (r, s - sign(s)))
    same_in = send(same, lambda r, s: (r, s - 2 * sign(s)))
    keep, swap = own_pieces(rest, im)
    swap_in = send(swap, lambda r, s: (r, s + sign(s)))
    moved = {}
    for step in (3, 2, 1):
        msg = merged(pos, keep, swap_in, same_in, other_in, step)
        moved[step] = send(msg, lambda r, s: (r + step * sign(s), s))
    acc = merged(pos, keep, swap_in, same_in, other_in, 0)
    for step in (1, 2, 3):
        acc = acc + moved[step].astype(F32)
    msg = acc[:, 16:].astype(BF16)
    acc = acc[:, :16] + send(msg, lambda r, s: (r + 4 * sign(s), s)).astype(F32)
    last = send(acc[1], lambda r, s: (r + sign(s), s + sign(s)))
    return (acc[0] + last)[None]


def solution(mesh):
    in_specs = (
        P("row", "col", None, None, None),
        P("row", "col", None),
        P("row", "col"),
        P("row", "col", None, None, None),
        P("row", "col", None),
    )
    out_specs = P("col", "row", None)
    return jax.shard_map(
        body, mesh=mesh, in_specs=in_specs, out_specs=out_specs, check_vma=False
    )
```

```python
import jax
import jax.numpy as jnp
from jax import lax
from jax.experimental import pallas as pl
from jax.experimental.pallas import tpu as pltpu
from jax.sharding import PartitionSpec as P


B = 64
ROWS = 16
COLS = 32
F32 = jnp.float32
BF16 = jnp.bfloat16


def joint(rule):
    pairs = []
    for r in range(ROWS):
        for s in range(COLS):
            r2, s2 = rule(r, s)
            pairs.append((r * COLS + s, (r2 % ROWS) * COLS + s2 % COLS))
    return pairs


def send(value, rule):
    return lax.ppermute(value, ("row", "col"), joint(rule))


def sign(s):
    return 1 if s % 2 == 0 else -1


def smem():
    return pl.BlockSpec(memory_space=pltpu.SMEM)


def vmem():
    return pl.BlockSpec(memory_space=pltpu.VMEM)


def budget(mib, flops, moved):
    return dict(
        compiler_params=pltpu.CompilerParams(vmem_limit_bytes=mib << 20),
        cost_estimate=pl.CostEstimate(flops=flops, bytes_accessed=moved, transcendentals=0),
    )


PART4 = 4 * 192 + 4 * 16
PART6 = 6 * 192 + 6 * 16


def column_of(pos_ref, blocks_ref, x, y, j):
    g = blocks_ref[x, y, j]
    return ((g // 4 - pos_ref[2] + 33) % 32) * 4 + g % 4


def pack(pos_ref, blocks_ref, p_ref, out_ref, n, x, y):
    for t in range(3):
        left = p_ref[(x * 4 + y) * 6 + 2 * t]
        right = p_ref[(x * 4 + y) * 6 + 2 * t + 1]
        at = 192 * n + 64 * t
        out_ref[at : at + 64, :] = jnp.concatenate([left, right], axis=1)
    row = lax.broadcasted_iota(jnp.int32, (16, 128), 0)
    table = jnp.zeros((16, 128), jnp.int32)
    for j in range(6):
        table = jnp.where(row == j, column_of(pos_ref, blocks_ref, x, y, j), table)
    out_ref[768 + 16 * n : 784 + 16 * n, :] = table.astype(F32).astype(BF16)


def expand(message_ref, n, tables_at, store):
    tables = message_ref[pl.ds(pl.multiple_of(tables_at + 16 * n, 16), 16), :]
    tiles = []
    for t in range(3):
        pair = message_ref[pl.ds(pl.multiple_of(192 * n + 64 * t, 64), 64), :]
        left, right = pair[:, 0:64], pair[:, 64:128]
        tiles.append(jnp.concatenate([left, left], axis=1))
        tiles.append(jnp.concatenate([right, right], axis=1))
    spots = [jnp.broadcast_to(tables[j : j + 1, :], (64, 128)) for j in range(6)]
    odd = (lax.broadcasted_iota(jnp.int32, (64, 128), 1) // 64).astype(F32)
    for m in range(6):
        column = (odd + 2.0 * m).astype(BF16)
        out = jnp.zeros((64, 128), BF16)
        for j in range(6):
            out = jnp.where(spots[j] == column, tiles[j], out)
        store(slice(128 * m, 128 * m + 128), out)


def pack_kernel(pos_ref, blocks_ref, p_ref, cross_ref, chip_ref):
    core = pos_ref[0]
    for x in range(4):
        pack(pos_ref, blocks_ref, p_ref, cross_ref, x, x, core * 3)
        pack(pos_ref, blocks_ref, p_ref, chip_ref, x, x, 3 - core * 3)


def packed(pos, blocks, tiles):
    return pl.pallas_call(
        pack_kernel,
        out_shape=(jax.ShapeDtypeStruct((PART4, 128), BF16),) * 2,
        in_specs=[smem(), smem(), vmem()],
        out_specs=(vmem(),) * 2,
        name="packed",
        **budget(4, 0, 2000000),
    )(pos, blocks, tiles)


def place_kernel(pos_ref, blocks_ref, p_ref, po_ref, up_ref, down_ref, inv_ref):
    for y in range(4):
        pack(pos_ref, blocks_ref, p_ref, up_ref, y, 3, y)
        pack(pos_ref, blocks_ref, p_ref, down_ref, y, 0, y)

    def prepare(b, carry):
        y, x = b // 4, b % 4
        for column in range(12):
            inv_ref[b * 12 + column] = 0
        for j in range(6):
            inv_ref[b * 12 + column_of(pos_ref, blocks_ref, x, y, j)] = j + 1
        return carry

    lax.fori_loop(0, 16, prepare, 0)

    def block(b, carry):
        y, x = b // 4, b % 4
        row = pl.multiple_of(b * B, B)

        def tile(column):
            j = inv_ref[b * 12 + column]
            value = p_ref[(x * 4 + y) * 6 + jnp.maximum(j - 1, 0)]
            return jnp.where(j > 0, value, jnp.zeros_like(value))

        for m in range(6):
            pair = jnp.concatenate([tile(2 * m), tile(2 * m + 1)], axis=1)
            po_ref[pl.ds(row, B), 128 * m : 128 * m + 128] = pair
        return carry

    lax.fori_loop(0, 16, block, 0)


def place(pos, blocks, tiles):
    return pl.pallas_call(
        place_kernel,
        out_shape=(
            jax.ShapeDtypeStruct((1024, 768), BF16),
            jax.ShapeDtypeStruct((PART4, 128), BF16),
            jax.ShapeDtypeStruct((PART4, 128), BF16),
        ),
        in_specs=[smem(), smem(), vmem()],
        out_specs=(vmem(),) * 3,
        scratch_shapes=[pltpu.SMEM((192,), jnp.int32)],
        name="place",
        **budget(4, 0, 2000000),
    )(pos, blocks, tiles)


def rim_kernel(up_own, down_own, cross_ref, chip_ref, up_ref, down_ref):
    for own, out, x in ((up_own, up_ref, 3), (down_own, down_ref, 0)):
        out[0:768, :] = own[0:768, :]
        out[1152:1216, :] = own[768:832, :]
        for n, ref in ((4, cross_ref), (5, chip_ref)):
            out[192 * n : 192 * n + 192, :] = ref[192 * x : 192 * x + 192, :]
            out[1152 + 16 * n : 1168 + 16 * n, :] = ref[768 + 16 * x : 784 + 16 * x, :]


def rims(*parts):
    return pl.pallas_call(
        rim_kernel,
        out_shape=(jax.ShapeDtypeStruct((PART6, 128), BF16),) * 2,
        in_specs=[vmem()] * 4,
        out_specs=(vmem(),) * 2,
        name="rims",
        **budget(4, 0, 2000000),
    )(*parts)


SLOTS = (
    ((1, 2), (None, None), (0, None)),
    ((0, 1), (2, None), (None, None)),
    ((None, 0), (1, 2), (None, None)),
    ((None, None), (0, 1), (None, 2)),
)


def dot(a, b):
    return jnp.dot(a, b, preferred_element_type=F32)


def local_kernel(
    pos_ref, codes_ref, live_ref, a_ref, po_ref, cross_ref, chip_ref,
    ad_ref, outer_ref, rest_ref, im_ref, side_ref, aidx_ref,
):
    core = pos_ref[0]
    r = pos_ref[1]

    def widen(x, carry):
        rows = pl.ds(pl.multiple_of(64 * x, 64), 64)
        for side, ref in ((core, cross_ref), (1 - core, chip_ref)):
            def store(cols, value):
                side_ref[side, rows, cols] = value

            expand(ref, x, 768, store)
        return carry

    lax.fori_loop(0, 4, widen, 0)

    def fill(b, carry):
        y = b // 4
        at = b % 4
        for k in range(9):
            aidx_ref[codes_ref[at, y, k]] = jnp.where(k < live_ref[at, y], k, -1)

        def tile(x, c):
            if c is None:
                return jnp.zeros((B, B), BF16)
            k = aidx_ref[c]
            value = a_ref[(x * 4 + y) * 9 + jnp.maximum(k, 0)]
            return jnp.where(k >= 0, value, jnp.zeros_like(value))

        for x in range(4):
            @pl.when(at == x)
            def _():
                for dy in range(3):
                    for m in range(3):
                        left, right = SLOTS[x][m]
                        left = None if left is None else left * 3 + dy
                        right = None if right is None else right * 3 + dy
                        pair = jnp.concatenate([tile(x, left), tile(x, right)], axis=1)
                        lane = 256 * dy + 128 * m if m < 2 else 768 + 128 * dy
                        ad_ref[y, 64 * x : 64 * x + 64, lane : lane + 128] = pair
        return carry

    lax.fori_loop(0, 16, fill, 0)

    for y in range(4):
        first = 1 if y == 0 else 0
        last = 1 if y == 3 else 2
        im_ref[256 * y : 256 * y + 256, :] = dot(
            ad_ref[y, :, 256 * first : 256 * last + 256],
            po_ref[256 * (y + first - 1) : 256 * (y + last), :],
        )

    windows = ((core * 2, 1 - core), (1 + core * 0, core), (2 - core * 2, 1 - core))
    for n, (window, kind) in enumerate(windows):
        lanes = pl.ds(pl.multiple_of(window * 256, 256), 256)
        for y in range(4):
            flipped = po_ref[256 * y : 256 * y + 256, lanes].T
            for o in range(16):
                shifted = (o - r - kind + 32) % 16
                flow = shifted // 8
                near = jnp.where(flow == 0, shifted, 15 - shifted)
                half = (flow + core) % 2
                spot = half * 8 + (near % 4) * 2 + near // 4
                row = pl.multiple_of(max(n - 1, 0) * 256 + spot * 16, 16)
                pt_ref = rest_ref if n else outer_ref
                pt_ref[pl.ds(row, 16), 256 * y : 256 * y + 256] = flipped[16 * o : 16 * o + 16, :]


def local_products(pos, codes, live, a, po, cross, chip):
    return pl.pallas_call(
        local_kernel,
        out_shape=(
            jax.ShapeDtypeStruct((4, 256, 1152), BF16),
            jax.ShapeDtypeStruct((256, 1024), BF16),
            jax.ShapeDtypeStruct((512, 1024), BF16),
            jax.ShapeDtypeStruct((1024, 768), F32),
            jax.ShapeDtypeStruct((2, 256, 768), BF16),
        ),
        in_specs=[smem(), smem(), smem()] + [vmem()] * 4,
        out_specs=(vmem(),) * 5,
        scratch_shapes=[pltpu.SMEM((9,), jnp.int32)],
        name="local_products",
        **budget(12, 1000000000, 12000000),
    )(pos, codes, live, a, po, cross, chip)


def pieces(pt_ref, base, im_ref, store):
    for chunk in range(5):
        k = slice(0, 256) if chunk == 0 else slice(768, 1024) if chunk == 4 else slice(0, 1024)
        cols = slice(256 * chunk, 256 * chunk + 256)
        store(cols, dot(pt_ref[base : base + 256, k], im_ref[k, cols]))


def halo_kernel(
    pos_ref, ad_ref, pt_ref, part_ref, side_ref, up_ref, down_ref,
    im_ref, same_ref, other_ref, hr_ref,
):
    core = pos_ref[0]

    def widen(n, carry):
        to = jnp.where(n < 4, n + 1, jnp.where(n == 4, core * 5, 5 - core * 5))
        for at, ref in ((0, up_ref), (64, down_ref)):
            def store(cols, value):
                hr_ref[to, at : at + 64, cols] = value

            expand(ref, n, 1152, store)
        return carry

    lax.fori_loop(0, 6, widen, 0)

    for y in range(4):
        rows = slice(256 * y, 256 * y + 256)
        first = 1 if y == 0 else 0
        last = 1 if y == 3 else 2
        count = last - first + 1
        total = part_ref[rows, :] + dot(
            ad_ref[y, :, 768 + 128 * first : 896 + 128 * last],
            hr_ref[y + first : y + last + 1].reshape(128 * count, 768),
        )
        if count == 3:
            im_ref[rows, 256:1024] = total.astype(BF16)
            continue
        dy, side, at = (0, 0, 0) if y == 0 else (2, 1, 5)
        edge = dot(ad_ref[y, :, 256 * dy : 256 * dy + 256], side_ref[side])
        edge = edge + dot(ad_ref[y, :, 768 + 128 * dy : 896 + 128 * dy], hr_ref[at])
        if y == 0:
            im_ref[rows, 0:256] = edge[:, 0:256].astype(BF16)
            im_ref[rows, 256:768] = (edge[:, 256:768] + total[:, 0:512]).astype(BF16)
            im_ref[rows, 768:1024] = total[:, 512:768].astype(BF16)
        else:
            im_ref[rows, 256:512] = total[:, 0:256].astype(BF16)
            im_ref[rows, 512:1024] = (edge[:, 0:512] + total[:, 256:768]).astype(BF16)
            im_ref[rows, 1024:1280] = edge[:, 512:768].astype(BF16)

    def store(cols, out):
        same_ref[:, cols] = out[0:128].astype(BF16)
        other_ref[:, cols] = out[128:256].astype(BF16)

    pieces(pt_ref, 0, im_ref, store)


def halo_products(pos, ad, pt, part, *halo):
    half = jax.ShapeDtypeStruct((128, 1280), BF16)
    return pl.pallas_call(
        halo_kernel,
        out_shape=(jax.ShapeDtypeStruct((1024, 1280), BF16), half, half),
        in_specs=[smem()] + [vmem()] * 6,
        out_specs=(vmem(),) * 3,
        scratch_shapes=[pltpu.VMEM((6, 128, 768), BF16)],
        name="halo_products",
        **budget(12, 1500000000, 12000000),
    )(pos, ad, pt, part, *halo)


def own_kernel(pt_ref, im_ref, keep_ref, swap_ref):
    for n in range(2):
        def store(cols, out):
            keep_ref[128 * n : 128 * n + 128, cols] = out[0:128]
            swap_ref[128 * n : 128 * n + 128, cols] = out[128:256].astype(BF16)

        pieces(pt_ref, 256 * n, im_ref, store)


def own_pieces(pt, im):
    return pl.pallas_call(
        own_kernel,
        out_shape=(
            jax.ShapeDtypeStruct((256, 1280), F32),
            jax.ShapeDtypeStruct((256, 1280), BF16),
        ),
        in_specs=[vmem(), vmem()],
        out_specs=(vmem(), vmem()),
        name="own_pieces",
        **budget(8, 1400000000, 6000000),
    )(pt, im)


def merge_kernel(
    pos_ref, keep_own, keep_partner, swap_own, swap_partner, same_ref, other_ref, out_ref, sum_ref
):
    def merge(low, high):
        def add(n, at, ref):
            sum_ref[n, :, at : at + 1280] += ref[...].astype(F32)

        zero = jnp.zeros((32, 256), F32)
        for n in range(2):
            for at in (0, 256, 1280, 1536):
                sum_ref[n, :, at : at + 256] = zero
        sum_ref[0, :, 256:1536] = keep_own[...]
        sum_ref[1, :, 256:1536] = swap_own[...].astype(F32)
        add(0, high, swap_partner)
        add(0, low, other_ref)
        add(1, low, keep_partner)
        add(1, high, same_ref)

    @pl.when(pos_ref[0] == 0)
    def _():
        merge(0, 512)

    @pl.when(pos_ref[0] == 1)
    def _():
        merge(512, 0)

    out_ref[...] = sum_ref[...].astype(out_ref.dtype)


def merged(pos, keep, swap, same, other, group):
    def rows(at):
        return pl.BlockSpec((32, 1280), lambda i: (at, 0))

    return pl.pallas_call(
        merge_kernel,
        grid=(1,),
        out_shape=jax.ShapeDtypeStruct((2, 32, 1792), F32 if group == 0 else BF16),
        in_specs=[smem()] + [rows(group), rows(group + 4)] * 2 + [rows(group)] * 2,
        out_specs=pl.BlockSpec((2, 32, 1792), lambda i: (0, 0, 0)),
        scratch_shapes=[pltpu.VMEM((2, 32, 1792), F32)],
        **budget(4, 0, 1000000),
    )(pos, keep, keep, swap, swap, same, other)


def body(operator_tiles, neighbour_codes, live_slots, prolong_tiles, coarse_blocks):
    r = lax.axis_index("row")
    s = lax.axis_index("col")
    core = s % 2
    pos = jnp.stack([core, r, s]).astype(jnp.int32)

    tiles = prolong_tiles.reshape(96, B, B)
    cross, chip = packed(pos, coarse_blocks, tiles)
    cross_in = send(cross, lambda r, s: (r, s - sign(s)))
    chip_in = send(chip, lambda r, s: (r, s + sign(s)))
    po, up_own, down_own = place(pos, coarse_blocks, tiles)
    up, down = rims(up_own, down_own, cross_in, chip_in)
    up_in = send(up, lambda r, s: (r + 1, s))
    down_in = send(down, lambda r, s: (r - 1, s))
    ad, outer, rest, part, side = local_products(
        pos, neighbour_codes, live_slots, operator_tiles.reshape(144, B, B), po, cross_in, chip_in
    )
    im, same, other = halo_products(pos, ad, outer, part, side, up_in, down_in)
    other_in = send(other, lambda r, s: (r, s - sign(s)))
    same_in = send(same, lambda r, s: (r, s - 2 * sign(s)))
    keep, swap = own_pieces(rest, im)
    swap_in = send(swap, lambda r, s: (r, s + sign(s)))
    moved = {}
    for step in (3, 2, 1):
        msg = merged(pos, keep, swap_in, same_in, other_in, step)
        moved[step] = send(msg, lambda r, s: (r + step * sign(s), s))
    acc = merged(pos, keep, swap_in, same_in, other_in, 0)
    for step in (1, 2, 3):
        acc = acc + moved[step].astype(F32)
    msg = acc[:, 16:].astype(BF16)
    acc = acc[:, :16] + send(msg, lambda r, s: (r + 4 * sign(s), s)).astype(F32)
    last = send(acc[1], lambda r, s: (r + sign(s), s + sign(s)))
    return (acc[0] + last)[None]


def solution(mesh):
    in_specs = (
        P("row", "col", None, None, None),
        P("row", "col", None),
        P("row", "col"),
        P("row", "col", None, None, None),
        P("row", "col", None),
    )
    out_specs = P("col", "row", None)
    return jax.shard_map(
        body, mesh=mesh, in_specs=in_specs, out_specs=out_specs, check_vma=False
    )
```

```python
import jax
import jax.numpy as jnp
from jax import lax
from jax.experimental import pallas as pl
from jax.experimental.pallas import tpu as pltpu
from jax.sharding import PartitionSpec as P


B = 64
ROWS = 16
COLS = 32
F32 = jnp.float32
BF16 = jnp.bfloat16


def joint(rule):
    pairs = []
    for r in range(ROWS):
        for s in range(COLS):
            r2, s2 = rule(r, s)
            pairs.append((r * COLS + s, (r2 % ROWS) * COLS + s2 % COLS))
    return pairs


def send(value, rule):
    return lax.ppermute(value, ("row", "col"), joint(rule))


def sign(s):
    return 1 if s % 2 == 0 else -1


def smem():
    return pl.BlockSpec(memory_space=pltpu.SMEM)


def vmem():
    return pl.BlockSpec(memory_space=pltpu.VMEM)


def budget(mib, flops, moved):
    return dict(
        compiler_params=pltpu.CompilerParams(vmem_limit_bytes=mib << 20),
        cost_estimate=pl.CostEstimate(flops=flops, bytes_accessed=moved, transcendentals=0),
    )


PART4 = 4 * 192 + 4 * 16
PART6 = 6 * 192 + 6 * 16


def column_of(pos_ref, blocks_ref, x, y, j):
    g = blocks_ref[x, y, j]
    return ((g // 4 - pos_ref[2] + 33) % 32) * 4 + g % 4


def pack(pos_ref, blocks_ref, p_ref, out_ref, n, x, y):
    for t in range(3):
        left = p_ref[(x * 4 + y) * 6 + 2 * t]
        right = p_ref[(x * 4 + y) * 6 + 2 * t + 1]
        at = 192 * n + 64 * t
        out_ref[at : at + 64, :] = jnp.concatenate([left, right], axis=1)
    row = lax.broadcasted_iota(jnp.int32, (16, 128), 0)
    table = jnp.zeros((16, 128), jnp.int32)
    for j in range(6):
        table = jnp.where(row == j, column_of(pos_ref, blocks_ref, x, y, j), table)
    out_ref[768 + 16 * n : 784 + 16 * n, :] = table.astype(F32).astype(BF16)


def expand(message_ref, n, tables_at, store):
    tables = message_ref[pl.ds(pl.multiple_of(tables_at + 16 * n, 16), 16), :]
    tiles = []
    for t in range(3):
        pair = message_ref[pl.ds(pl.multiple_of(192 * n + 64 * t, 64), 64), :]
        left, right = pair[:, 0:64], pair[:, 64:128]
        tiles.append(jnp.concatenate([left, left], axis=1))
        tiles.append(jnp.concatenate([right, right], axis=1))
    spots = [jnp.broadcast_to(tables[j : j + 1, :], (64, 128)) for j in range(6)]
    odd = (lax.broadcasted_iota(jnp.int32, (64, 128), 1) // 64).astype(F32)
    for m in range(6):
        column = (odd + 2.0 * m).astype(BF16)
        out = jnp.zeros((64, 128), BF16)
        for j in range(6):
            out = jnp.where(spots[j] == column, tiles[j], out)
        store(slice(128 * m, 128 * m + 128), out)


def pack_kernel(pos_ref, blocks_ref, p_ref, cross_ref, chip_ref):
    core = pos_ref[0]
    for x in range(4):
        pack(pos_ref, blocks_ref, p_ref, cross_ref, x, x, core * 3)
        pack(pos_ref, blocks_ref, p_ref, chip_ref, x, x, 3 - core * 3)


def packed(kernel, pos, blocks, tiles):
    return pl.pallas_call(
        kernel,
        out_shape=(jax.ShapeDtypeStruct((PART4, 128), BF16),) * 2,
        in_specs=[smem(), smem(), vmem()],
        out_specs=(vmem(),) * 2,
        **budget(4, 0, 2000000),
    )(pos, blocks, tiles)


def row_kernel(pos_ref, blocks_ref, p_ref, up_ref, down_ref):
    for y in range(4):
        pack(pos_ref, blocks_ref, p_ref, up_ref, y, 3, y)
        pack(pos_ref, blocks_ref, p_ref, down_ref, y, 0, y)


def place_kernel(pos_ref, blocks_ref, p_ref, po_ref, inv_ref):
    def prepare(b, carry):
        y, x = b // 4, b % 4
        for column in range(12):
            inv_ref[b * 12 + column] = 0
        for j in range(6):
            inv_ref[b * 12 + column_of(pos_ref, blocks_ref, x, y, j)] = j + 1
        return carry

    lax.fori_loop(0, 16, prepare, 0)

    def block(b, carry):
        y, x = b // 4, b % 4
        row = pl.multiple_of(b * B, B)

        def tile(column):
            j = inv_ref[b * 12 + column]
            value = p_ref[(x * 4 + y) * 6 + jnp.maximum(j - 1, 0)]
            return jnp.where(j > 0, value, jnp.zeros_like(value))

        for m in range(6):
            pair = jnp.concatenate([tile(2 * m), tile(2 * m + 1)], axis=1)
            po_ref[pl.ds(row, B), 128 * m : 128 * m + 128] = pair
        return carry

    lax.fori_loop(0, 16, block, 0)


def place(pos, blocks, tiles):
    return pl.pallas_call(
        place_kernel,
        out_shape=jax.ShapeDtypeStruct((1024, 768), BF16),
        in_specs=[smem(), smem(), vmem()],
        out_specs=vmem(),
        scratch_shapes=[pltpu.SMEM((192,), jnp.int32)],
        name="place",
        **budget(4, 0, 2000000),
    )(pos, blocks, tiles)


def rim_kernel(up_own, down_own, cross_ref, chip_ref, up_ref, down_ref):
    for own, out, x in ((up_own, up_ref, 3), (down_own, down_ref, 0)):
        out[0:768, :] = own[0:768, :]
        out[1152:1216, :] = own[768:832, :]
        for n, ref in ((4, cross_ref), (5, chip_ref)):
            out[192 * n : 192 * n + 192, :] = ref[192 * x : 192 * x + 192, :]
            out[1152 + 16 * n : 1168 + 16 * n, :] = ref[768 + 16 * x : 784 + 16 * x, :]


def rims(*parts):
    return pl.pallas_call(
        rim_kernel,
        out_shape=(jax.ShapeDtypeStruct((PART6, 128), BF16),) * 2,
        in_specs=[vmem()] * 4,
        out_specs=(vmem(),) * 2,
        name="rims",
        **budget(4, 0, 2000000),
    )(*parts)


SLOTS = (
    ((1, 2), (None, None), (0, None)),
    ((0, 1), (2, None), (None, None)),
    ((None, 0), (1, 2), (None, None)),
    ((None, None), (0, 1), (None, 2)),
)


def dot(a, b):
    return jnp.dot(a, b, preferred_element_type=F32)


def local_kernel(
    pos_ref, codes_ref, live_ref, a_ref, po_ref, cross_ref, chip_ref,
    ad_ref, outer_ref, rest_ref, im_ref, side_ref, aidx_ref,
):
    core = pos_ref[0]
    r = pos_ref[1]

    def widen(x, carry):
        rows = pl.ds(pl.multiple_of(64 * x, 64), 64)
        for side, ref in ((core, cross_ref), (1 - core, chip_ref)):
            def store(cols, value):
                side_ref[side, rows, cols] = value

            expand(ref, x, 768, store)
        return carry

    lax.fori_loop(0, 4, widen, 0)

    def fill(b, carry):
        y = b // 4
        at = b % 4
        for k in range(9):
            aidx_ref[codes_ref[at, y, k]] = jnp.where(k < live_ref[at, y], k, -1)

        def tile(x, c):
            if c is None:
                return jnp.zeros((B, B), BF16)
            k = aidx_ref[c]
            value = a_ref[(x * 4 + y) * 9 + jnp.maximum(k, 0)]
            return jnp.where(k >= 0, value, jnp.zeros_like(value))

        for x in range(4):
            @pl.when(at == x)
            def _():
                for dy in range(3):
                    for m in range(3):
                        left, right = SLOTS[x][m]
                        left = None if left is None else left * 3 + dy
                        right = None if right is None else right * 3 + dy
                        pair = jnp.concatenate([tile(x, left), tile(x, right)], axis=1)
                        lane = 256 * dy + 128 * m if m < 2 else 768 + 128 * dy
                        ad_ref[y, 64 * x : 64 * x + 64, lane : lane + 128] = pair
        return carry

    lax.fori_loop(0, 16, fill, 0)

    for y in range(4):
        first = 1 if y == 0 else 0
        last = 1 if y == 3 else 2
        im_ref[256 * y : 256 * y + 256, :] = dot(
            ad_ref[y, :, 256 * first : 256 * last + 256],
            po_ref[256 * (y + first - 1) : 256 * (y + last), :],
        )

    windows = ((core * 2, 1 - core), (1 + core * 0, core), (2 - core * 2, 1 - core))
    for n, (window, kind) in enumerate(windows):
        lanes = pl.ds(pl.multiple_of(window * 256, 256), 256)
        for y in range(4):
            flipped = po_ref[256 * y : 256 * y + 256, lanes].T
            for o in range(16):
                shifted = (o - r - kind + 32) % 16
                flow = shifted // 8
                near = jnp.where(flow == 0, shifted, 15 - shifted)
                half = (flow + core) % 2
                spot = half * 8 + (near & 1) * 4 + (near & 2) + (near >> 2)
                row = pl.multiple_of(max(n - 1, 0) * 256 + spot * 16, 16)
                pt_ref = rest_ref if n else outer_ref
                pt_ref[pl.ds(row, 16), 256 * y : 256 * y + 256] = flipped[16 * o : 16 * o + 16, :]


def local_products(pos, codes, live, a, po, cross, chip):
    return pl.pallas_call(
        local_kernel,
        out_shape=(
            jax.ShapeDtypeStruct((4, 256, 1152), BF16),
            jax.ShapeDtypeStruct((256, 1024), BF16),
            jax.ShapeDtypeStruct((512, 1024), BF16),
            jax.ShapeDtypeStruct((1024, 768), F32),
            jax.ShapeDtypeStruct((2, 256, 768), BF16),
        ),
        in_specs=[smem(), smem(), smem()] + [vmem()] * 4,
        out_specs=(vmem(),) * 5,
        scratch_shapes=[pltpu.SMEM((9,), jnp.int32)],
        name="local_products",
        **budget(12, 1000000000, 12000000),
    )(pos, codes, live, a, po, cross, chip)


def pieces(pt_ref, base, im_ref, store):
    for chunk in range(5):
        k = slice(0, 256) if chunk == 0 else slice(768, 1024) if chunk == 4 else slice(0, 1024)
        cols = slice(256 * chunk, 256 * chunk + 256)
        store(cols, dot(pt_ref[base : base + 256, k], im_ref[k, cols]))


def halo_kernel(
    pos_ref, ad_ref, pt_ref, part_ref, side_ref, up_ref, down_ref,
    im_ref, same_ref, other_ref, hr_ref,
):
    core = pos_ref[0]

    def widen(n, carry):
        to = jnp.where(n < 4, n + 1, jnp.where(n == 4, core * 5, 5 - core * 5))
        for at, ref in ((0, up_ref), (64, down_ref)):
            def store(cols, value):
                hr_ref[to, at : at + 64, cols] = value

            expand(ref, n, 1152, store)
        return carry

    lax.fori_loop(0, 6, widen, 0)

    for y in range(4):
        rows = slice(256 * y, 256 * y + 256)
        first = 1 if y == 0 else 0
        last = 1 if y == 3 else 2
        count = last - first + 1
        total = part_ref[rows, :] + dot(
            ad_ref[y, :, 768 + 128 * first : 896 + 128 * last],
            hr_ref[y + first : y + last + 1].reshape(128 * count, 768),
        )
        if count == 3:
            im_ref[rows, 256:1024] = total.astype(BF16)
            continue
        dy, side, at = (0, 0, 0) if y == 0 else (2, 1, 5)
        edge = dot(ad_ref[y, :, 256 * dy : 256 * dy + 256], side_ref[side])
        edge = edge + dot(ad_ref[y, :, 768 + 128 * dy : 896 + 128 * dy], hr_ref[at])
        if y == 0:
            im_ref[rows, 0:256] = edge[:, 0:256].astype(BF16)
            im_ref[rows, 256:768] = (edge[:, 256:768] + total[:, 0:512]).astype(BF16)
            im_ref[rows, 768:1024] = total[:, 512:768].astype(BF16)
        else:
            im_ref[rows, 256:512] = total[:, 0:256].astype(BF16)
            im_ref[rows, 512:1024] = (edge[:, 0:512] + total[:, 256:768]).astype(BF16)
            im_ref[rows, 1024:1280] = edge[:, 512:768].astype(BF16)

    def store(cols, out):
        same_ref[:, cols] = out[0:128].astype(BF16)
        other_ref[:, cols] = out[128:256].astype(BF16)

    pieces(pt_ref, 0, im_ref, store)


def halo_products(pos, ad, pt, part, *halo):
    half = jax.ShapeDtypeStruct((128, 1280), BF16)
    return pl.pallas_call(
        halo_kernel,
        out_shape=(jax.ShapeDtypeStruct((1024, 1280), BF16), half, half),
        in_specs=[smem()] + [vmem()] * 6,
        out_specs=(vmem(),) * 3,
        scratch_shapes=[pltpu.VMEM((6, 128, 768), BF16)],
        name="halo_products",
        **budget(12, 1500000000, 12000000),
    )(pos, ad, pt, part, *halo)


def own_kernel(pt_ref, im_ref, keep_ref, swap_ref):
    for n in range(2):
        def store(cols, out):
            keep_ref[128 * n : 128 * n + 128, cols] = out[0:128]
            swap_ref[128 * n : 128 * n + 128, cols] = out[128:256].astype(BF16)

        pieces(pt_ref, 256 * n, im_ref, store)


def own_pieces(pt, im):
    return pl.pallas_call(
        own_kernel,
        out_shape=(
            jax.ShapeDtypeStruct((256, 1280), F32),
            jax.ShapeDtypeStruct((256, 1280), BF16),
        ),
        in_specs=[vmem(), vmem()],
        out_specs=(vmem(), vmem()),
        name="own_pieces",
        **budget(8, 1400000000, 6000000),
    )(pt, im)


def merge_kernel(pos_ref, low_ref, middle_ref, high_ref, out_ref, sum_ref):
    zero = jnp.zeros((64, 256), F32)
    for at in (0, 1536):
        sum_ref[:, at : at + 256] = zero
    sum_ref[:, 256:1536] = middle_ref[...].astype(F32)

    def add(low, high):
        sum_ref[:, 0:1280] += low[...].astype(F32)
        sum_ref[:, 512:1792] += high[...].astype(F32)

    @pl.when(pos_ref[0] == 0)
    def _():
        add(low_ref, high_ref)

    @pl.when(pos_ref[0] == 1)
    def _():
        add(high_ref, low_ref)

    out_ref[...] = sum_ref[...].astype(out_ref.dtype)


def merged(pos, low, middle, high, dtype):
    parts = (low, middle, high)

    def rows(at):
        return pl.BlockSpec((64, 1280), lambda i: (at, 0))

    return pl.pallas_call(
        merge_kernel,
        grid=(1,),
        out_shape=jax.ShapeDtypeStruct((64, 1792), dtype),
        in_specs=[smem()] + [rows(at) for _, at in parts],
        out_specs=pl.BlockSpec((64, 1792), lambda i: (0, 0)),
        scratch_shapes=[pltpu.VMEM((64, 1792), F32)],
        **budget(4, 0, 1000000),
    )(pos, *(array for array, _ in parts))


def body(operator_tiles, neighbour_codes, live_slots, prolong_tiles, coarse_blocks):
    r = lax.axis_index("row")
    s = lax.axis_index("col")
    core = s % 2
    pos = jnp.stack([core, r, s]).astype(jnp.int32)

    tiles = prolong_tiles.reshape(96, B, B)
    cross, chip = packed(pack_kernel, pos, coarse_blocks, tiles)
    cross_in = send(cross, lambda r, s: (r, s - sign(s)))
    chip_in = send(chip, lambda r, s: (r, s + sign(s)))
    up_own, down_own = packed(row_kernel, pos, coarse_blocks, tiles)
    up, down = rims(up_own, down_own, cross_in, chip_in)
    up_in = send(up, lambda r, s: (r + 1, s))
    down_in = send(down, lambda r, s: (r - 1, s))
    po = place(pos, coarse_blocks, tiles)
    ad, outer, rest, part, side = local_products(
        pos, neighbour_codes, live_slots, operator_tiles.reshape(144, B, B), po, cross_in, chip_in
    )
    im, same, other = halo_products(pos, ad, outer, part, side, up_in, down_in)
    other_in = send(other, lambda r, s: (r, s - sign(s)))
    same_in = send(same, lambda r, s: (r, s - 2 * sign(s)))
    keep, swap = own_pieces(rest, im)
    swap_in = send(swap, lambda r, s: (r, s + sign(s)))
    other_slab = ((keep, 2), (swap_in, 0), (same_in, 0))
    own_slab = ((other_in, 0), (keep, 0), (swap_in, 2))

    def later(parts):
        return tuple((array, at + 1) for array, at in parts)

    def hop(step, value):
        return send(value, lambda r, s: (r + step * sign(s), s)).astype(F32)

    first = {}
    kept = {}
    for label, parts in (("p", other_slab), ("o", own_slab)):
        first[label] = hop(1, merged(pos, *later(parts), BF16))
    for label, parts in (("p", other_slab), ("o", own_slab)):
        kept[label] = merged(pos, *parts, F32)
    total = {}
    for label in ("p", "o"):
        got = first[label]
        acc = kept[label]
        for step, size in ((2, 32), (4, 16)):
            moved = hop(step, (acc[size:] + got[size:]).astype(BF16))
            acc = acc[:size] + got[:size]
            got = moved
        total[label] = acc + got
    last = send(total["p"], lambda r, s: (r + sign(s), s + sign(s)))
    return (total["o"] + last)[None]


def solution(mesh):
    in_specs = (
        P("row", "col", None, None, None),
        P("row", "col", None),
        P("row", "col"),
        P("row", "col", None, None, None),
        P("row", "col", None),
    )
    out_specs = P("col", "row", None)
    return jax.shard_map(
        body, mesh=mesh, in_specs=in_specs, out_specs=out_specs, check_vma=False
    )
```

```python
import jax
import jax.numpy as jnp
from jax import lax
from jax.experimental import pallas as pl
from jax.experimental.pallas import tpu as pltpu
from jax.sharding import PartitionSpec as P


B = 64
ROWS = 16
COLS = 32
F32 = jnp.float32
BF16 = jnp.bfloat16


def joint(rule):
    pairs = []
    for r in range(ROWS):
        for s in range(COLS):
            r2, s2 = rule(r, s)
            pairs.append((r * COLS + s, (r2 % ROWS) * COLS + s2 % COLS))
    return pairs


def send(value, rule):
    return lax.ppermute(value, ("row", "col"), joint(rule))


def sign(s):
    return 1 if s % 2 == 0 else -1


def smem():
    return pl.BlockSpec(memory_space=pltpu.SMEM)


def vmem():
    return pl.BlockSpec(memory_space=pltpu.VMEM)


def budget(mib, flops, moved):
    return dict(
        compiler_params=pltpu.CompilerParams(vmem_limit_bytes=mib << 20),
        cost_estimate=pl.CostEstimate(flops=flops, bytes_accessed=moved, transcendentals=0),
    )


PART4 = 4 * 192 + 4 * 16
PART6 = 6 * 192 + 6 * 16


def column_of(pos_ref, x, y, j):
    g = pos_ref[3 + (x * 4 + y) * 6 + j]
    return (((g >> 2) - pos_ref[2] + 33) & 31) * 4 + (g & 3)


def pack(pos_ref, p_ref, out_ref, n, x, y):
    for t in range(3):
        left = p_ref[(x * 4 + y) * 6 + 2 * t]
        right = p_ref[(x * 4 + y) * 6 + 2 * t + 1]
        at = 192 * n + 64 * t
        out_ref[at : at + 64, :] = jnp.concatenate([left, right], axis=1)
    row = lax.broadcasted_iota(jnp.int32, (16, 128), 0)
    table = jnp.zeros((16, 128), jnp.int32)
    for j in range(6):
        table = jnp.where(row == j, column_of(pos_ref, x, y, j), table)
    out_ref[768 + 16 * n : 784 + 16 * n, :] = table.astype(F32).astype(BF16)


def expand(message_ref, n, tables_at, store):
    tables = message_ref[pl.ds(pl.multiple_of(tables_at + 16 * n, 16), 16), :]
    tiles = []
    for t in range(3):
        pair = message_ref[pl.ds(pl.multiple_of(192 * n + 64 * t, 64), 64), :]
        left, right = pair[:, 0:64], pair[:, 64:128]
        tiles.append(jnp.concatenate([left, left], axis=1))
        tiles.append(jnp.concatenate([right, right], axis=1))
    spots = [jnp.broadcast_to(tables[j : j + 1, :], (64, 128)) for j in range(6)]
    spread(tiles, spots, store)


def spread(tiles, spots, store):
    odd = (lax.broadcasted_iota(jnp.int32, (64, 128), 1) // 64).astype(F32)
    for m in range(6):
        column = (odd + 2.0 * m).astype(BF16)
        out = jnp.zeros((64, 128), BF16)
        for j in range(6):
            out = jnp.where(spots[j] == column, tiles[j], out)
        store(slice(128 * m, 128 * m + 128), out)


def pack_kernel(pos_ref, p_ref, cross_ref, chip_ref):
    core = pos_ref[0]
    for x in range(4):
        pack(pos_ref, p_ref, cross_ref, x, x, core * 3)
        pack(pos_ref, p_ref, chip_ref, x, x, 3 - core * 3)


def packed(kernel, pos, tiles):
    return pl.pallas_call(
        kernel,
        out_shape=(jax.ShapeDtypeStruct((PART4, 128), BF16),) * 2,
        in_specs=[smem(), vmem()],
        out_specs=(vmem(),) * 2,
        **budget(4, 0, 2000000),
    )(pos, tiles)


def row_kernel(pos_ref, p_ref, up_ref, down_ref):
    for y in range(4):
        pack(pos_ref, p_ref, up_ref, y, 3, y)
        pack(pos_ref, p_ref, down_ref, y, 0, y)


def place_kernel(pos_ref, p_ref, po_ref):
    def block(b, carry):
        y, x = b >> 2, b & 3
        rows = pl.ds(pl.multiple_of(b * B, B), B)
        tiles = []
        spots = []
        for j in range(6):
            tile = p_ref[(x * 4 + y) * 6 + j]
            tiles.append(jnp.concatenate([tile, tile], axis=1))
            spots.append(jnp.full((64, 128), column_of(pos_ref, x, y, j).astype(F32)).astype(BF16))

        def store(cols, value):
            po_ref[rows, cols] = value

        spread(tiles, spots, store)
        return carry

    lax.fori_loop(0, 16, block, 0)


def place(pos, tiles):
    return pl.pallas_call(
        place_kernel,
        out_shape=jax.ShapeDtypeStruct((1024, 768), BF16),
        in_specs=[smem(), vmem()],
        out_specs=vmem(),
        name="place",
        **budget(4, 0, 2000000),
    )(pos, tiles)


def rim_kernel(up_own, down_own, cross_ref, chip_ref, up_ref, down_ref):
    for own, out, x in ((up_own, up_ref, 3), (down_own, down_ref, 0)):
        out[0:768, :] = own[0:768, :]
        out[1152:1216, :] = own[768:832, :]
        for n, ref in ((4, cross_ref), (5, chip_ref)):
            out[192 * n : 192 * n + 192, :] = ref[192 * x : 192 * x + 192, :]
            out[1152 + 16 * n : 1168 + 16 * n, :] = ref[768 + 16 * x : 784 + 16 * x, :]


def rims(*parts):
    return pl.pallas_call(
        rim_kernel,
        out_shape=(jax.ShapeDtypeStruct((PART6, 128), BF16),) * 2,
        in_specs=[vmem()] * 4,
        out_specs=(vmem(),) * 2,
        name="rims",
        **budget(4, 0, 2000000),
    )(*parts)


SLOTS = (
    ((1, 2), (None, None), (0, None)),
    ((0, 1), (2, None), (None, None)),
    ((None, 0), (1, 2), (None, None)),
    ((None, None), (0, 1), (None, 2)),
)


def dot(a, b):
    return jnp.dot(a, b, preferred_element_type=F32)


def local_kernel(
    pos_ref, codes_ref, live_ref, a_ref, po_ref, cross_ref, chip_ref,
    ad_ref, outer_ref, rest_ref, im_ref, side_ref, aidx_ref,
):
    core = pos_ref[0]
    r = pos_ref[1]

    def widen(x, carry):
        rows = pl.ds(pl.multiple_of(64 * x, 64), 64)
        for side, ref in ((core, cross_ref), (1 - core, chip_ref)):
            def store(cols, value):
                side_ref[side, rows, cols] = value

            expand(ref, x, 768, store)
        return carry

    lax.fori_loop(0, 4, widen, 0)

    def fill(b, carry):
        y = b >> 2
        at = b & 3
        for k in range(9):
            aidx_ref[codes_ref[at, y, k]] = jnp.where(k < live_ref[at, y], k, -1)

        def tile(x, c):
            if c is None:
                return jnp.zeros((B, B), BF16)
            k = aidx_ref[c]
            value = a_ref[(x * 4 + y) * 9 + jnp.maximum(k, 0)]
            return jnp.where(k >= 0, value, jnp.zeros_like(value))

        for x in range(4):
            @pl.when(at == x)
            def _():
                for dy in range(3):
                    for m in range(3):
                        left, right = SLOTS[x][m]
                        left = None if left is None else left * 3 + dy
                        right = None if right is None else right * 3 + dy
                        pair = jnp.concatenate([tile(x, left), tile(x, right)], axis=1)
                        lane = 256 * dy + 128 * m if m < 2 else 768 + 128 * dy
                        ad_ref[y, 64 * x : 64 * x + 64, lane : lane + 128] = pair
        return carry

    lax.fori_loop(0, 16, fill, 0)

    for y in range(4):
        first = 1 if y == 0 else 0
        last = 1 if y == 3 else 2
        im_ref[256 * y : 256 * y + 256, :] = dot(
            ad_ref[y, :, 256 * first : 256 * last + 256],
            po_ref[256 * (y + first - 1) : 256 * (y + last), :],
        )

    windows = ((core * 2, 1 - core), (1 + core * 0, core), (2 - core * 2, 1 - core))
    for n, (window, kind) in enumerate(windows):
        lanes = pl.ds(pl.multiple_of(window * 256, 256), 256)
        for y in range(4):
            flipped = po_ref[256 * y : 256 * y + 256, lanes].T
            for o in range(16):
                shifted = (o - r - kind + 32) & 15
                flow = shifted >> 3
                near = jnp.where(flow == 0, shifted, 15 - shifted)
                half = (flow + core) & 1
                spot = half * 8 + (near & 1) * 4 + (near & 2) + (near >> 2)
                row = pl.multiple_of(max(n - 1, 0) * 256 + spot * 16, 16)
                pt_ref = rest_ref if n else outer_ref
                pt_ref[pl.ds(row, 16), 256 * y : 256 * y + 256] = flipped[16 * o : 16 * o + 16, :]


def local_products(pos, codes, live, a, po, cross, chip):
    return pl.pallas_call(
        local_kernel,
        out_shape=(
            jax.ShapeDtypeStruct((4, 256, 1152), BF16),
            jax.ShapeDtypeStruct((256, 1024), BF16),
            jax.ShapeDtypeStruct((512, 1024), BF16),
            jax.ShapeDtypeStruct((1024, 768), F32),
            jax.ShapeDtypeStruct((2, 256, 768), BF16),
        ),
        in_specs=[smem(), smem(), smem()] + [vmem()] * 4,
        out_specs=(vmem(),) * 5,
        scratch_shapes=[pltpu.SMEM((9,), jnp.int32)],
        name="local_products",
        **budget(12, 1000000000, 12000000),
    )(pos, codes, live, a, po, cross, chip)


def pieces(pt_ref, base, im_ref, store):
    for chunk in range(5):
        k = slice(0, 256) if chunk == 0 else slice(768, 1024) if chunk == 4 else slice(0, 1024)
        cols = slice(256 * chunk, 256 * chunk + 256)
        store(cols, dot(pt_ref[base : base + 256, k], im_ref[k, cols]))


def halo_kernel(
    pos_ref, ad_ref, pt_ref, part_ref, side_ref, up_ref, down_ref,
    im_ref, same_ref, other_ref, hr_ref,
):
    core = pos_ref[0]

    def widen(n, carry):
        to = jnp.where(n < 4, n + 1, jnp.where(n == 4, core * 5, 5 - core * 5))
        for at, ref in ((0, up_ref), (64, down_ref)):
            def store(cols, value):
                hr_ref[to, at : at + 64, cols] = value

            expand(ref, n, 1152, store)
        return carry

    lax.fori_loop(0, 6, widen, 0)

    for y in range(4):
        rows = slice(256 * y, 256 * y + 256)
        first = 1 if y == 0 else 0
        last = 1 if y == 3 else 2
        count = last - first + 1
        total = part_ref[rows, :] + dot(
            ad_ref[y, :, 768 + 128 * first : 896 + 128 * last],
            hr_ref[y + first : y + last + 1].reshape(128 * count, 768),
        )
        if count == 3:
            im_ref[rows, 256:1024] = total.astype(BF16)
            continue
        dy, side, at = (0, 0, 0) if y == 0 else (2, 1, 5)
        edge = dot(ad_ref[y, :, 256 * dy : 256 * dy + 256], side_ref[side])
        edge = edge + dot(ad_ref[y, :, 768 + 128 * dy : 896 + 128 * dy], hr_ref[at])
        if y == 0:
            im_ref[rows, 0:256] = edge[:, 0:256].astype(BF16)
            im_ref[rows, 256:768] = (edge[:, 256:768] + total[:, 0:512]).astype(BF16)
            im_ref[rows, 768:1024] = total[:, 512:768].astype(BF16)
        else:
            im_ref[rows, 256:512] = total[:, 0:256].astype(BF16)
            im_ref[rows, 512:1024] = (edge[:, 0:512] + total[:, 256:768]).astype(BF16)
            im_ref[rows, 1024:1280] = edge[:, 512:768].astype(BF16)

    def store(cols, out):
        same_ref[:, cols] = out[0:128].astype(BF16)
        other_ref[:, cols] = out[128:256].astype(BF16)

    pieces(pt_ref, 0, im_ref, store)


def halo_products(pos, ad, pt, part, *halo):
    half = jax.ShapeDtypeStruct((128, 1280), BF16)
    return pl.pallas_call(
        halo_kernel,
        out_shape=(jax.ShapeDtypeStruct((1024, 1280), BF16), half, half),
        in_specs=[smem()] + [vmem()] * 6,
        out_specs=(vmem(),) * 3,
        scratch_shapes=[pltpu.VMEM((6, 128, 768), BF16)],
        name="halo_products",
        **budget(12, 1500000000, 12000000),
    )(pos, ad, pt, part, *halo)


def own_kernel(pt_ref, im_ref, keep_ref, swap_ref):
    for n in range(2):
        def store(cols, out):
            keep_ref[128 * n : 128 * n + 128, cols] = out[0:128]
            swap_ref[128 * n : 128 * n + 128, cols] = out[128:256].astype(BF16)

        pieces(pt_ref, 256 * n, im_ref, store)


def own_pieces(pt, im):
    return pl.pallas_call(
        own_kernel,
        out_shape=(
            jax.ShapeDtypeStruct((256, 1280), F32),
            jax.ShapeDtypeStruct((256, 1280), BF16),
        ),
        in_specs=[vmem(), vmem()],
        out_specs=(vmem(), vmem()),
        name="own_pieces",
        **budget(8, 1400000000, 6000000),
    )(pt, im)


def merge_kernel(pos_ref, low_ref, middle_ref, high_ref, out_ref, sum_ref):
    zero = jnp.zeros((64, 256), F32)
    for at in (0, 1536):
        sum_ref[:, at : at + 256] = zero
    sum_ref[:, 256:1536] = middle_ref[...].astype(F32)

    def add(low, high):
        sum_ref[:, 0:1280] += low[...].astype(F32)
        sum_ref[:, 512:1792] += high[...].astype(F32)

    @pl.when(pos_ref[0] == 0)
    def _():
        add(low_ref, high_ref)

    @pl.when(pos_ref[0] == 1)
    def _():
        add(high_ref, low_ref)

    out_ref[...] = sum_ref[...].astype(out_ref.dtype)


def merged(pos, low, middle, high, dtype):
    parts = (low, middle, high)

    def rows(at):
        return pl.BlockSpec((64, 1280), lambda i: (at, 0))

    return pl.pallas_call(
        merge_kernel,
        grid=(1,),
        out_shape=jax.ShapeDtypeStruct((64, 1792), dtype),
        in_specs=[smem()] + [rows(at) for _, at in parts],
        out_specs=pl.BlockSpec((64, 1792), lambda i: (0, 0)),
        scratch_shapes=[pltpu.VMEM((64, 1792), F32)],
        **budget(4, 0, 1000000),
    )(pos, *(array for array, _ in parts))


def body(operator_tiles, neighbour_codes, live_slots, prolong_tiles, coarse_blocks):
    r = lax.axis_index("row")
    s = lax.axis_index("col")
    core = s % 2
    pos = jnp.concatenate([jnp.stack([core, r, s]).astype(jnp.int32), coarse_blocks.reshape(96)])

    tiles = prolong_tiles.reshape(96, B, B)
    cross, chip = packed(pack_kernel, pos, tiles)
    cross_in = send(cross, lambda r, s: (r, s - sign(s)))
    chip_in = send(chip, lambda r, s: (r, s + sign(s)))
    up_own, down_own = packed(row_kernel, pos, tiles)
    up, down = rims(up_own, down_own, cross_in, chip_in)
    up_in = send(up, lambda r, s: (r + 1, s))
    down_in = send(down, lambda r, s: (r - 1, s))
    po = place(pos, tiles)
    ad, outer, rest, part, side = local_products(
        pos, neighbour_codes, live_slots, operator_tiles.reshape(144, B, B), po, cross_in, chip_in
    )
    im, same, other = halo_products(pos, ad, outer, part, side, up_in, down_in)
    other_in = send(other, lambda r, s: (r, s - sign(s)))
    same_in = send(same, lambda r, s: (r, s - 2 * sign(s)))
    keep, swap = own_pieces(rest, im)
    swap_in = send(swap, lambda r, s: (r, s + sign(s)))
    other_slab = ((keep, 2), (swap_in, 0), (same_in, 0))
    own_slab = ((other_in, 0), (keep, 0), (swap_in, 2))

    def later(parts):
        return tuple((array, at + 1) for array, at in parts)

    def hop(step, value):
        return send(value, lambda r, s: (r + step * sign(s), s)).astype(F32)

    first = {}
    kept = {}
    for label, parts in (("p", other_slab), ("o", own_slab)):
        first[label] = hop(1, merged(pos, *later(parts), BF16))
    for label, parts in (("p", other_slab), ("o", own_slab)):
        kept[label] = merged(pos, *parts, F32)
    total = {}
    for label in ("p", "o"):
        got = first[label]
        acc = kept[label]
        for step, size in ((2, 32), (4, 16)):
            moved = hop(step, (acc[size:] + got[size:]).astype(BF16))
            acc = acc[:size] + got[:size]
            got = moved
        total[label] = acc + got
    last = send(total["p"], lambda r, s: (r + sign(s), s + sign(s)))
    return (total["o"] + last)[None]


def solution(mesh):
    in_specs = (
        P("row", "col", None, None, None),
        P("row", "col", None),
        P("row", "col"),
        P("row", "col", None, None, None),
        P("row", "col", None),
    )
    out_specs = P("col", "row", None)
    return jax.shard_map(
        body, mesh=mesh, in_specs=in_specs, out_specs=out_specs, check_vma=False
    )
```

```python
import jax
import jax.numpy as jnp
from jax import lax
from jax.experimental import pallas as pl
from jax.experimental.pallas import tpu as pltpu
from jax.sharding import PartitionSpec as P


B = 64
ROWS = 16
COLS = 32
F32 = jnp.float32
BF16 = jnp.bfloat16


def joint(rule):
    pairs = []
    for r in range(ROWS):
        for s in range(COLS):
            r2, s2 = rule(r, s)
            pairs.append((r * COLS + s, (r2 % ROWS) * COLS + s2 % COLS))
    return pairs


def send(value, rule):
    return lax.ppermute(value, ("row", "col"), joint(rule))


def sign(s):
    return 1 if s % 2 == 0 else -1


def smem():
    return pl.BlockSpec(memory_space=pltpu.SMEM)


def vmem():
    return pl.BlockSpec(memory_space=pltpu.VMEM)


def budget(mib, flops, moved):
    return dict(
        compiler_params=pltpu.CompilerParams(vmem_limit_bytes=mib << 20),
        cost_estimate=pl.CostEstimate(flops=flops, bytes_accessed=moved, transcendentals=0),
    )


PART4 = 4 * 192 + 4 * 16
PART6 = 6 * 192 + 6 * 16


def column_of(pos_ref, x, y, j):
    g = pos_ref[3 + (x * 4 + y) * 6 + j]
    return (((g >> 2) - pos_ref[2] + 33) & 31) * 4 + (g & 3)


def pack(pos_ref, p_ref, out_ref, n, x, y, at_y=None):
    at_y = y if at_y is None else at_y
    for t in range(3):
        left = p_ref[(x * 4 + at_y) * 6 + 2 * t]
        right = p_ref[(x * 4 + at_y) * 6 + 2 * t + 1]
        at = 192 * n + 64 * t
        out_ref[at : at + 64, :] = jnp.concatenate([left, right], axis=1)
    row = lax.broadcasted_iota(jnp.int32, (16, 128), 0)
    table = jnp.zeros((16, 128), jnp.int32)
    for j in range(6):
        table = jnp.where(row == j, column_of(pos_ref, x, y, j), table)
    out_ref[768 + 16 * n : 784 + 16 * n, :] = table.astype(F32).astype(BF16)


def expand(message_ref, n, tables_at, store):
    tables = message_ref[pl.ds(pl.multiple_of(tables_at + 16 * n, 16), 16), :]
    tiles = []
    for t in range(3):
        pair = message_ref[pl.ds(pl.multiple_of(192 * n + 64 * t, 64), 64), :]
        left, right = pair[:, 0:64], pair[:, 64:128]
        tiles.append(jnp.concatenate([left, left], axis=1))
        tiles.append(jnp.concatenate([right, right], axis=1))
    spots = [jnp.broadcast_to(tables[j : j + 1, :], (64, 128)) for j in range(6)]
    spread(tiles, spots, store)


def spread(tiles, spots, store):
    odd = (lax.broadcasted_iota(jnp.int32, (64, 128), 1) // 64).astype(F32)
    for m in range(6):
        column = (odd + 2.0 * m).astype(BF16)
        out = jnp.zeros((64, 128), BF16)
        for j in range(6):
            out = jnp.where(spots[j] == column, tiles[j], out)
        store(slice(128 * m, 128 * m + 128), out)


def pack_kernel(pos_ref, p_ref, cross_ref, chip_ref, buf_ref, sems):
    core = pos_ref[0]
    copies = []
    for side, y in enumerate((core * 3, 3 - core * 3)):
        for x in range(4):
            copies.append(
                pltpu.make_async_copy(
                    p_ref.at[pl.ds((x * 4 + y) * 6, 6)],
                    buf_ref.at[pl.ds((x * 4 + side) * 6, 6)],
                    sems.at[side * 4 + x],
                )
            )
            copies[-1].start()
    for side, (y, ref) in enumerate(((core * 3, cross_ref), (3 - core * 3, chip_ref))):
        for x in range(4):
            copies[side * 4 + x].wait()
            pack(pos_ref, buf_ref, ref, x, x, y, side)


def packed(kernel, pos, tiles, own_copies=False):
    return pl.pallas_call(
        kernel,
        out_shape=(jax.ShapeDtypeStruct((PART4, 128), BF16),) * 2,
        in_specs=[smem(), pl.BlockSpec(memory_space=pltpu.HBM) if own_copies else vmem()],
        out_specs=(vmem(),) * 2,
        scratch_shapes=[
            pltpu.VMEM((96, B, B), BF16),
            pltpu.SemaphoreType.DMA((8,)),
        ]
        if own_copies
        else [],
        **budget(4, 0, 2000000),
    )(pos, pltpu.with_memory_space_constraint(tiles, pltpu.HBM) if own_copies else tiles)


def row_kernel(pos_ref, p_ref, up_ref, down_ref):
    for y in range(4):
        pack(pos_ref, p_ref, up_ref, y, 3, y)
        pack(pos_ref, p_ref, down_ref, y, 0, y)


def place_kernel(pos_ref, p_ref, po_ref):
    def block(b, carry):
        y, x = b >> 2, b & 3
        rows = pl.ds(pl.multiple_of(b * B, B), B)
        tiles = []
        spots = []
        for j in range(6):
            tile = p_ref[(x * 4 + y) * 6 + j]
            tiles.append(jnp.concatenate([tile, tile], axis=1))
            spots.append(jnp.full((64, 128), column_of(pos_ref, x, y, j).astype(F32)).astype(BF16))

        def store(cols, value):
            po_ref[rows, cols] = value

        spread(tiles, spots, store)
        return carry

    lax.fori_loop(0, 16, block, 0)


def place(pos, tiles):
    return pl.pallas_call(
        place_kernel,
        out_shape=jax.ShapeDtypeStruct((1024, 768), BF16),
        in_specs=[smem(), vmem()],
        out_specs=vmem(),
        name="place",
        **budget(4, 0, 2000000),
    )(pos, tiles)


def rim_kernel(up_own, down_own, cross_ref, chip_ref, up_ref, down_ref):
    for own, out, x in ((up_own, up_ref, 3), (down_own, down_ref, 0)):
        out[0:768, :] = own[0:768, :]
        out[1152:1216, :] = own[768:832, :]
        for n, ref in ((4, cross_ref), (5, chip_ref)):
            out[192 * n : 192 * n + 192, :] = ref[192 * x : 192 * x + 192, :]
            out[1152 + 16 * n : 1168 + 16 * n, :] = ref[768 + 16 * x : 784 + 16 * x, :]


def rims(*parts):
    return pl.pallas_call(
        rim_kernel,
        out_shape=(jax.ShapeDtypeStruct((PART6, 128), BF16),) * 2,
        in_specs=[vmem()] * 4,
        out_specs=(vmem(),) * 2,
        name="rims",
        **budget(4, 0, 2000000),
    )(*parts)


SLOTS = (
    ((1, 2), (None, None), (0, None)),
    ((0, 1), (2, None), (None, None)),
    ((None, 0), (1, 2), (None, None)),
    ((None, None), (0, 1), (None, 2)),
)


def dot(a, b):
    return jnp.dot(a, b, preferred_element_type=F32)


def local_kernel(
    pos_ref, codes_ref, live_ref, a_ref, po_ref, cross_ref, chip_ref,
    ad_ref, outer_ref, rest_ref, im_ref, side_ref, aidx_ref,
):
    core = pos_ref[0]
    r = pos_ref[1]

    def widen(x, carry):
        rows = pl.ds(pl.multiple_of(64 * x, 64), 64)
        for side, ref in ((core, cross_ref), (1 - core, chip_ref)):
            def store(cols, value):
                side_ref[side, rows, cols] = value

            expand(ref, x, 768, store)
        return carry

    lax.fori_loop(0, 4, widen, 0)

    def fill(b, carry):
        y = b >> 2
        at = b & 3
        for k in range(9):
            aidx_ref[codes_ref[at, y, k]] = jnp.where(k < live_ref[at, y], k, -1)

        def tile(x, c):
            if c is None:
                return jnp.zeros((B, B), BF16)
            k = aidx_ref[c]
            value = a_ref[(x * 4 + y) * 9 + jnp.maximum(k, 0)]
            return jnp.where(k >= 0, value, jnp.zeros_like(value))

        for x in range(4):
            @pl.when(at == x)
            def _():
                for dy in range(3):
                    for m in range(3):
                        left, right = SLOTS[x][m]
                        left = None if left is None else left * 3 + dy
                        right = None if right is None else right * 3 + dy
                        pair = jnp.concatenate([tile(x, left), tile(x, right)], axis=1)
                        lane = 256 * dy + 128 * m if m < 2 else 768 + 128 * dy
                        ad_ref[y, 64 * x : 64 * x + 64, lane : lane + 128] = pair
        return carry

    lax.fori_loop(0, 16, fill, 0)

    for y in range(4):
        first = 1 if y == 0 else 0
        last = 1 if y == 3 else 2
        im_ref[256 * y : 256 * y + 256, :] = dot(
            ad_ref[y, :, 256 * first : 256 * last + 256],
            po_ref[256 * (y + first - 1) : 256 * (y + last), :],
        )

    windows = ((core * 2, 1 - core), (1 + core * 0, core), (2 - core * 2, 1 - core))
    for n, (window, kind) in enumerate(windows):
        lanes = pl.ds(pl.multiple_of(window * 256, 256), 256)
        for y in range(4):
            flipped = po_ref[256 * y : 256 * y + 256, lanes].T
            for o in range(16):
                shifted = (o - r - kind + 32) & 15
                flow = shifted >> 3
                near = jnp.where(flow == 0, shifted, 15 - shifted)
                half = (flow + core) & 1
                spot = half * 8 + (near & 1) * 4 + (near & 2) + (near >> 2)
                row = pl.multiple_of(max(n - 1, 0) * 256 + spot * 16, 16)
                pt_ref = rest_ref if n else outer_ref
                pt_ref[pl.ds(row, 16), 256 * y : 256 * y + 256] = flipped[16 * o : 16 * o + 16, :]


def local_products(pos, codes, live, a, po, cross, chip):
    return pl.pallas_call(
        local_kernel,
        out_shape=(
            jax.ShapeDtypeStruct((4, 256, 1152), BF16),
            jax.ShapeDtypeStruct((256, 1024), BF16),
            jax.ShapeDtypeStruct((512, 1024), BF16),
            jax.ShapeDtypeStruct((1024, 768), F32),
            jax.ShapeDtypeStruct((2, 256, 768), BF16),
        ),
        in_specs=[smem(), smem(), smem()] + [vmem()] * 4,
        out_specs=(vmem(),) * 5,
        scratch_shapes=[pltpu.SMEM((9,), jnp.int32)],
        name="local_products",
        **budget(12, 1000000000, 12000000),
    )(pos, codes, live, a, po, cross, chip)


def pieces(pt_ref, base, im_ref, store):
    for chunk in range(5):
        k = slice(0, 256) if chunk == 0 else slice(768, 1024) if chunk == 4 else slice(0, 1024)
        cols = slice(256 * chunk, 256 * chunk + 256)
        store(cols, dot(pt_ref[base : base + 256, k], im_ref[k, cols]))


def halo_kernel(
    pos_ref, ad_ref, pt_ref, part_ref, side_ref, up_ref, down_ref,
    im_ref, same_ref, other_ref, hr_ref,
):
    core = pos_ref[0]

    def widen(n, carry):
        to = jnp.where(n < 4, n + 1, jnp.where(n == 4, core * 5, 5 - core * 5))
        for at, ref in ((0, up_ref), (64, down_ref)):
            def store(cols, value):
                hr_ref[to, at : at + 64, cols] = value

            expand(ref, n, 1152, store)
        return carry

    lax.fori_loop(0, 6, widen, 0)

    for y in range(4):
        rows = slice(256 * y, 256 * y + 256)
        first = 1 if y == 0 else 0
        last = 1 if y == 3 else 2
        count = last - first + 1
        total = part_ref[rows, :] + dot(
            ad_ref[y, :, 768 + 128 * first : 896 + 128 * last],
            hr_ref[y + first : y + last + 1].reshape(128 * count, 768),
        )
        if count == 3:
            im_ref[rows, 256:1024] = total.astype(BF16)
            continue
        dy, side, at = (0, 0, 0) if y == 0 else (2, 1, 5)
        edge = dot(ad_ref[y, :, 256 * dy : 256 * dy + 256], side_ref[side])
        edge = edge + dot(ad_ref[y, :, 768 + 128 * dy : 896 + 128 * dy], hr_ref[at])
        if y == 0:
            im_ref[rows, 0:256] = edge[:, 0:256].astype(BF16)
            im_ref[rows, 256:768] = (edge[:, 256:768] + total[:, 0:512]).astype(BF16)
            im_ref[rows, 768:1024] = total[:, 512:768].astype(BF16)
        else:
            im_ref[rows, 256:512] = total[:, 0:256].astype(BF16)
            im_ref[rows, 512:1024] = (edge[:, 0:512] + total[:, 256:768]).astype(BF16)
            im_ref[rows, 1024:1280] = edge[:, 512:768].astype(BF16)

    def store(cols, out):
        same_ref[:, cols] = out[0:128].astype(BF16)
        other_ref[:, cols] = out[128:256].astype(BF16)

    pieces(pt_ref, 0, im_ref, store)


def halo_products(pos, ad, pt, part, *halo):
    half = jax.ShapeDtypeStruct((128, 1280), BF16)
    return pl.pallas_call(
        halo_kernel,
        out_shape=(jax.ShapeDtypeStruct((1024, 1280), BF16), half, half),
        in_specs=[smem()] + [vmem()] * 6,
        out_specs=(vmem(),) * 3,
        scratch_shapes=[pltpu.VMEM((6, 128, 768), BF16)],
        name="halo_products",
        **budget(12, 1500000000, 12000000),
    )(pos, ad, pt, part, *halo)


def own_kernel(pt_ref, im_ref, keep_ref, swap_ref):
    for n in range(2):
        def store(cols, out):
            keep_ref[128 * n : 128 * n + 128, cols] = out[0:128]
            swap_ref[128 * n : 128 * n + 128, cols] = out[128:256].astype(BF16)

        pieces(pt_ref, 256 * n, im_ref, store)


def own_pieces(pt, im):
    return pl.pallas_call(
        own_kernel,
        out_shape=(
            jax.ShapeDtypeStruct((256, 1280), F32),
            jax.ShapeDtypeStruct((256, 1280), BF16),
        ),
        in_specs=[vmem(), vmem()],
        out_specs=(vmem(), vmem()),
        name="own_pieces",
        **budget(8, 1400000000, 6000000),
    )(pt, im)


def merge_kernel(pos_ref, low_ref, middle_ref, high_ref, out_ref, sum_ref):
    zero = jnp.zeros((64, 256), F32)
    for at in (0, 1536):
        sum_ref[:, at : at + 256] = zero
    sum_ref[:, 256:1536] = middle_ref[...].astype(F32)

    def add(low, high):
        sum_ref[:, 0:1280] += low[...].astype(F32)
        sum_ref[:, 512:1792] += high[...].astype(F32)

    @pl.when(pos_ref[0] == 0)
    def _():
        add(low_ref, high_ref)

    @pl.when(pos_ref[0] == 1)
    def _():
        add(high_ref, low_ref)

    out_ref[...] = sum_ref[...].astype(out_ref.dtype)


def merged(pos, low, middle, high, dtype):
    parts = (low, middle, high)

    def rows(at):
        return pl.BlockSpec((64, 1280), lambda i: (at, 0))

    return pl.pallas_call(
        merge_kernel,
        grid=(1,),
        out_shape=jax.ShapeDtypeStruct((64, 1792), dtype),
        in_specs=[smem()] + [rows(at) for _, at in parts],
        out_specs=pl.BlockSpec((64, 1792), lambda i: (0, 0)),
        scratch_shapes=[pltpu.VMEM((64, 1792), F32)],
        **budget(4, 0, 1000000),
    )(pos, *(array for array, _ in parts))


def body(operator_tiles, neighbour_codes, live_slots, prolong_tiles, coarse_blocks):
    r = lax.axis_index("row")
    s = lax.axis_index("col")
    core = s % 2
    pos = jnp.concatenate([jnp.stack([core, r, s]).astype(jnp.int32), coarse_blocks.reshape(96)])

    tiles = prolong_tiles.reshape(96, B, B)
    cross, chip = packed(pack_kernel, pos, tiles, True)
    cross_in = send(cross, lambda r, s: (r, s - sign(s)))
    chip_in = send(chip, lambda r, s: (r, s + sign(s)))
    up_own, down_own = packed(row_kernel, pos, tiles)
    up, down = rims(up_own, down_own, cross_in, chip_in)
    up_in = send(up, lambda r, s: (r + 1, s))
    down_in = send(down, lambda r, s: (r - 1, s))
    po = place(pos, tiles)
    ad, outer, rest, part, side = local_products(
        pos, neighbour_codes, live_slots, operator_tiles.reshape(144, B, B), po, cross_in, chip_in
    )
    im, same, other = halo_products(pos, ad, outer, part, side, up_in, down_in)
    other_in = send(other, lambda r, s: (r, s - sign(s)))
    same_in = send(same, lambda r, s: (r, s - 2 * sign(s)))
    keep, swap = own_pieces(rest, im)
    swap_in = send(swap, lambda r, s: (r, s + sign(s)))
    other_slab = ((keep, 2), (swap_in, 0), (same_in, 0))
    own_slab = ((other_in, 0), (keep, 0), (swap_in, 2))

    def later(parts):
        return tuple((array, at + 1) for array, at in parts)

    def hop(step, value):
        return send(value, lambda r, s: (r + step * sign(s), s)).astype(F32)

    first = {}
    kept = {}
    for label, parts in (("p", other_slab), ("o", own_slab)):
        first[label] = hop(1, merged(pos, *later(parts), BF16))
    for label, parts in (("p", other_slab), ("o", own_slab)):
        kept[label] = merged(pos, *parts, F32)
    total = {}
    for label in ("p", "o"):
        got = first[label]
        acc = kept[label]
        for step, size in ((2, 32), (4, 16)):
            moved = hop(step, (acc[size:] + got[size:]).astype(BF16))
            acc = acc[:size] + got[:size]
            got = moved
        total[label] = acc + got
    last = send(total["p"], lambda r, s: (r + sign(s), s + sign(s)))
    return (total["o"] + last)[None]


def solution(mesh):
    in_specs = (
        P("row", "col", None, None, None),
        P("row", "col", None),
        P("row", "col"),
        P("row", "col", None, None, None),
        P("row", "col", None),
    )
    out_specs = P("col", "row", None)
    return jax.shard_map(body, mesh=mesh, in_specs=in_specs, out_specs=out_specs, check_vma=False)
```
